256 devices in a mesh: sub: 8 (over z), row: 2 (over core), col: 16 (over y, x).
Axes of the slice: x: 4, y: 4, z: 8, core: 2. Of those that a mesh axis runs over, the one named last changes fastest.
Arguments:
- factor_cols: bfloat16 [8, 2, 2048, 4096], P('sub', None, 'col', 'row'), may hold values from -0.09375 to 0.09375
- block_pattern: int32 [8, 16, 16], P('sub'), may hold values 0 or 1
- diag_inverse: float32 [8, 4096, 2048], P('sub', ('row', 'col')), may hold values from -1 to 2
- coupling_cols: bfloat16 [8, 2, 2048, 1024], P('sub', 'row', 'col'), may hold values from -0.09375 to 0.09375
- separator_rows: int32 [8, 1024], P('sub'), may hold values from 0 to 1535, as said below
- root_inverse: float32 [1536, 1536], P('col'), may hold values from -1 to 2
- right_side: float32 [8, 4096, 128], P('sub', 'row'), may hold values from -6 to 6
- root_right: float32 [1536, 128], P('col'), may hold values from -6 to 6
Outputs:
- solution: float32 [8, 4096, 128], P('sub', ('row', 'col'))
- root_solution: float32 [1536, 128], P('col')
The draws below stay inside these ranges and needn't reach their ends.
Inputs may be any that keep to these rules, and one draw needn't show every extreme that they name: `separator_rows`: within one section the 1024 entries are distinct.
All inputs are finite; a program needn't handle non-finite values. No bound on the sum of `block_pattern` on one device may be relied on, other than what follows from the above.
Results may differ from the reference program's by a relative error of at most 0.003.
Values may be sent and summed in bfloat16 or wider, within the bound.
No kernel may reach another device: no remote copies, remote signals or barrier semaphores. Data moves between devices by JAX's collectives and lax.ppermute only.
A program may use at most 64 MiB of HBM per device.

```python
import jax
import jax.numpy as jnp
from jax import lax

BLOCK = 256
SOURCES = 128
SEPARATOR = 1536
COUPLED = 1024
PANEL = 2048
PANELS = 2
SECTION = 4096
BLOCKS = 16
SECTIONS = 8


def inverse_blocks(key, count, order):
    noise = jnp.clip(jax.random.normal(key, (count, order, order), jnp.float32), -6.0, 6.0)
    return jnp.eye(order, dtype=jnp.float32)[None] + 0.3 * noise / jnp.sqrt(order * 1.0)


def draw_diag_inverse(key, part):
    blocks = inverse_blocks(jax.random.fold_in(key, 11), SECTIONS * PANELS, PANEL)
    return blocks.reshape(SECTIONS, SECTION, PANEL)


def draw_root_inverse(key, part):
    return inverse_blocks(jax.random.fold_in(key, 13), 1, SEPARATOR)[0]


def draw_separator_rows(key, part):

    def one_section(section_key):
        first_key, second_key = jax.random.split(section_key)
        inner = jax.random.permutation(first_key, SEPARATOR - 2)[:COUPLED - 2] + 1
        values = jnp.concatenate([jnp.array([0, SEPARATOR - 1], jnp.int32), inner.astype(jnp.int32)])
        return values[jax.random.permutation(second_key, COUPLED)]
    return jax.vmap(one_section)(jax.random.split(jax.random.fold_in(key, 17), SECTIONS))


def place_ends(values, stream_key, low, top_value):
    place = [jax.random.randint(jax.random.fold_in(stream_key, axis), (), 0, length) for axis, length in enumerate(values.shape)]
    widest = values.shape.index(max(values.shape))
    beside = place[:widest] + [(place[widest] + 1) % values.shape[widest]] + place[widest + 1:]
    return values.at[tuple(place)].set(low).at[tuple(beside)].set(top_value)


def steps_of(own_key, extent, cuts, smallest, high):
    loudness = 1.0
    for axis_at, shards_of in cuts:
        heights = jax.random.uniform(jax.random.fold_in(jax.random.fold_in(own_key, 6), axis_at), (shards_of,), jnp.float32, smallest / len(cuts), high / len(cuts))
        loudness = loudness * jnp.repeat(jnp.exp(heights), extent[axis_at] // shards_of).reshape((-1,) + (1,) * (len(extent) - 1 - axis_at))
    return loudness


def normal_values(key, dims, width, most, shards=(), kind=jnp.bfloat16):
    entries = jax.random.normal(key, dims, jnp.float32) * width
    if len(shards) > 0:
        entries = steps_of(key, dims, shards, -0.22, 0.18) * entries
    return jnp.clip(entries, min=-most, max=most).astype(kind)


def setup_inputs(seed: int = 0) -> dict:
    seeds = jax.random.split(jax.random.key(seed), 9)
    factor_cols = normal_values(seeds[0], (SECTIONS, PANELS, PANEL, SECTION), SECTION ** -0.5, 0.09375, ((0, 8), (2, 16), (3, 2)))
    block_pattern = place_ends((jax.random.randint(seeds[1], (SECTIONS, BLOCKS, BLOCKS), 0, 3) < 2).astype(jnp.int32), jax.random.fold_in(seeds[1], 1), 0, 1)
    diag_inverse = draw_diag_inverse(jax.random.fold_in(seeds[8], 71), 0)
    coupling_cols = normal_values(seeds[3], (SECTIONS, PANELS, PANEL, COUPLED), SECTION ** -0.5, 0.09375, ((0, 8), (1, 2), (2, 16)))
    separator_rows = draw_separator_rows(jax.random.fold_in(seeds[8], 71), 0)
    root_inverse = draw_root_inverse(jax.random.fold_in(seeds[8], 71), 0)
    right_side = normal_values(seeds[6], (SECTIONS, SECTION, SOURCES), 1.0, 6.0, ((0, 8), (1, 2)), jnp.float32)
    root_right = normal_values(seeds[7], (SEPARATOR, SOURCES), 1.0, 6.0, ((0, 16),), jnp.float32)
    return {"factor_cols": factor_cols, "block_pattern": block_pattern, "diag_inverse": diag_inverse, "coupling_cols": coupling_cols, "separator_rows": separator_rows, "root_inverse": root_inverse, "right_side": right_side, "root_right": root_right}


precise = lax.Precision.HIGHEST


def reference(factor_cols, block_pattern, diag_inverse, coupling_cols, separator_rows, root_inverse, right_side, root_right):
    positions = jnp.arange(SECTION)
    row_panels = positions // PANEL
    below_all = row_panels[:, None] > row_panels[None, :]
    separator_ids = jnp.arange(SEPARATOR)
    mapped_total = jnp.zeros((SEPARATOR, SOURCES), jnp.float32)
    kept = []
    for section in range(SECTIONS):
        expanded = jnp.repeat(jnp.repeat(block_pattern[section], BLOCK, axis=0), BLOCK, axis=1)
        lower_mask = jnp.where(below_all, expanded, 0).astype(jnp.bfloat16)
        masked_cols = factor_cols[section].reshape(SECTION, SECTION) * lower_mask.T
        coupled = coupling_cols[section].reshape(SECTION, COUPLED)
        solved_parts = []
        rounded_parts = []
        for current in range(PANELS):
            rows_now = slice(current * PANEL, (current + 1) * PANEL)
            panel_total = jnp.zeros((PANEL, SOURCES), jnp.float32)
            for earlier in range(current):
                cols_then = slice(earlier * PANEL, (earlier + 1) * PANEL)
                panel_total = panel_total + jnp.dot(masked_cols[cols_then, rows_now].T, rounded_parts[earlier], preferred_element_type=jnp.float32)
            solved = jnp.dot(diag_inverse[section, rows_now], right_side[section, rows_now] - panel_total, precision=precise, preferred_element_type=jnp.float32)
            solved_parts.append(solved)
            rounded_parts.append(solved.astype(jnp.bfloat16))
        rounded_all = jnp.concatenate(rounded_parts, axis=0)
        onehot = (separator_ids[:, None] == separator_rows[section][None, :]).astype(jnp.float32)
        contribution = jnp.dot(coupled.T, rounded_all, preferred_element_type=jnp.float32)
        mapped_total = mapped_total + jnp.dot(onehot, contribution, precision=precise, preferred_element_type=jnp.float32)
        kept.append((section, masked_cols, coupled, onehot, solved_parts))
    root_half = jnp.dot(root_inverse, root_right - mapped_total, precision=precise, preferred_element_type=jnp.float32)
    root_solution = jnp.dot(root_inverse.T, root_half, precision=precise, preferred_element_type=jnp.float32)
    outputs = []
    for section, masked_cols, coupled, onehot, solved_parts in kept:
        picked = jnp.dot(onehot.T, root_solution, precision=precise, preferred_element_type=jnp.float32).astype(jnp.bfloat16)
        couple_back = jnp.dot(coupled, picked, preferred_element_type=jnp.float32)
        finished = [None] * PANELS
        finished_low = [None] * PANELS
        for current in range(PANELS - 1, -1, -1):
            rows_now = slice(current * PANEL, (current + 1) * PANEL)
            panel_total = couple_back[rows_now]
            for later in range(current + 1, PANELS):
                rows_later = slice(later * PANEL, (later + 1) * PANEL)
                panel_total = panel_total + jnp.dot(masked_cols[rows_now, rows_later], finished_low[later], preferred_element_type=jnp.float32)
            value = jnp.dot(diag_inverse[section, rows_now].T, solved_parts[current] - panel_total, precision=precise, preferred_element_type=jnp.float32)
            finished[current] = value
            finished_low[current] = value.astype(jnp.bfloat16)
        outputs.append(jnp.concatenate(finished, axis=0))
    return jnp.stack(outputs), root_solution
```

```python
import jax
import jax.numpy as jnp
from jax import lax
from jax.sharding import PartitionSpec as P

BLOCK = 256
PANEL = 2048
SEPARATOR = 1536
COLS = 16
SUBS = 8

f32 = jnp.float32
bf16 = jnp.bfloat16
fine = lax.Precision.HIGH
first_axes = (((0,), (0,)), ((), ()))


def mul(left, right, **kw):
    return jnp.dot(left, right, preferred_element_type=f32, **kw)


def mul_t(left, right, **kw):
    return lax.dot_general(left, right, first_axes, preferred_element_type=f32, **kw)


def sum_scatter(partial, axes, count):
    parts = partial.reshape(count, -1, partial.shape[-1])
    return lax.all_to_all(parts, axes, 0, 0).astype(f32).sum(0)


def gather(chunk, axes, count):
    spread = jnp.broadcast_to(chunk[None], (count,) + chunk.shape)
    return lax.all_to_all(spread, axes, 0, 0)


def shards(
    factor_cols,
    block_pattern,
    diag_inverse,
    coupling_cols,
    separator_rows,
    root_inverse,
    right_side,
    root_right,
):
    table = block_pattern[0]
    inverse = diag_inverse[0]
    couple = coupling_cols[0, 0]
    rows_sep = separator_rows[0]
    row_id = lax.axis_index("row")
    col_id = lax.axis_index("col")
    sources = right_side.shape[-1]

    blocks = lax.dynamic_slice(table, (PANEL // BLOCK, col_id // 2), (PANEL // BLOCK, 1))
    lower = factor_cols[0, 0] * jnp.repeat(blocks[:, 0], BLOCK)[None, :].astype(bf16)

    onehot = (rows_sep[:, None] == jnp.arange(SEPARATOR)[None, :]).astype(bf16)
    couple_sep = mul(couple, onehot).astype(bf16)

    own = mul(inverse, right_side[0], precision=fine)
    first_low = lax.ppermute(own.astype(bf16), "row", [(0, 1)])
    total = sum_scatter(mul_t(lower, first_low).astype(bf16), "col", COLS)
    total = gather(total.astype(bf16), "col", COLS).reshape(PANEL, sources)
    solved = own - mul(inverse, total.astype(f32), precision=fine)

    updates = sum_scatter(mul_t(couple_sep, solved.astype(bf16)), ("col", "row"), COLS * 2)
    updates = gather(updates, "sub", SUBS).sum(0)
    half = updates.shape[0]
    rhs = lax.dynamic_slice_in_dim(root_right, row_id * half, half, 0) - updates
    rhs = gather(rhs, ("col", "row"), COLS * 2).reshape(SEPARATOR, sources)
    root_half = mul(root_inverse, rhs, precision=fine)
    root_part = sum_scatter(mul_t(root_inverse, root_half, precision=fine), "col", COLS)
    root_full = gather(root_part.astype(bf16), "col", COLS).reshape(SEPARATOR, sources)

    value = solved - mul(couple_sep, root_full)
    value = sum_scatter(mul_t(inverse, value, precision=fine), "col", COLS)
    later_low = gather(value.astype(bf16), "col", COLS).reshape(PANEL, sources)
    terms = lax.ppermute(mul(lower, later_low), "row", [(1, 0)])
    value = value - sum_scatter(mul_t(inverse, terms, precision=fine), "col", COLS)
    return value[None], root_part


def solution(mesh):
    return jax.shard_map(
        shards,
        mesh=mesh,
        in_specs=(
            P("sub", None, "col", "row"),
            P("sub", None, None),
            P("sub", ("row", "col"), None),
            P("sub", "row", "col", None),
            P("sub", None),
            P("col", None),
            P("sub", "row", None),
            P("col", None),
        ),
        out_specs=(P("sub", ("row", "col"), None), P("col", None)),
        check_vma=False,
    )
```

```python
import jax
import jax.numpy as jnp
from jax import lax
from jax.sharding import PartitionSpec as P

BLOCK = 256
PANEL = 2048
SEPARATOR = 1536
COLS = 16
SUBS = 8

f32 = jnp.float32
bf16 = jnp.bfloat16
fine = lax.Precision.HIGH
first_axes = (((0,), (0,)), ((), ()))


def mul(left, right, **kw):
    return jnp.dot(left, right, preferred_element_type=f32, **kw)


def mul_t(left, right, **kw):
    return lax.dot_general(left, right, first_axes, preferred_element_type=f32, **kw)


def sum_scatter(partial, axes, count):
    parts = partial.reshape(count, -1, partial.shape[-1])
    here = lax.axis_index(axes)
    own = lax.dynamic_index_in_dim(parts, here, 0)
    others = lax.all_to_all(parts.astype(bf16), axes, 0, 0).astype(f32)
    index = lax.broadcasted_iota(jnp.int32, (count, 1, 1), 0)
    return jnp.where(index == here, own, others).sum(0)


def gather(chunk, axes, count):
    spread = jnp.broadcast_to(chunk[None], (count,) + chunk.shape)
    return lax.all_to_all(spread, axes, 0, 0)


def shards(
    factor_cols,
    block_pattern,
    diag_inverse,
    coupling_cols,
    separator_rows,
    root_inverse,
    right_side,
    root_right,
):
    table = block_pattern[0]
    inverse = diag_inverse[0]
    couple = coupling_cols[0, 0]
    rows_sep = separator_rows[0]
    row_id = lax.axis_index("row")
    col_id = lax.axis_index("col")
    sources = right_side.shape[-1]

    blocks = lax.dynamic_slice(table, (PANEL // BLOCK, col_id // 2), (PANEL // BLOCK, 1))
    lower = factor_cols[0, 0] * jnp.repeat(blocks[:, 0], BLOCK)[None, :].astype(bf16)

    share = root_inverse.shape[0]
    half = SEPARATOR // 2
    lane = lax.broadcasted_iota(jnp.int32, root_inverse.shape, 1)
    line = lax.broadcasted_iota(jnp.int32, root_inverse.shape, 0) + col_id * share
    on_diag = lane == line
    diag = jnp.where(on_diag, root_inverse, 0.0).sum(1, keepdims=True)
    pieces = []
    rest = diag
    for _ in range(3):
        pieces.append(lax.reduce_precision(rest, 8, 7))
        rest = rest - pieces[-1]
    off = lax.dynamic_slice_in_dim(jnp.where(on_diag, 0.0, root_inverse), row_id * half, half, 1)
    packed = jnp.concatenate([off] + pieces + [jnp.zeros((share, 125), f32)], 1).astype(bf16)
    packed = lax.all_gather(packed, "col", axis=0, tiled=True)

    onehot = (jnp.arange(SEPARATOR)[:, None] == rows_sep[None, :]).astype(bf16)
    couple_sep = lax.dot_general(
        onehot, couple, (((1,), (1,)), ((), ())), preferred_element_type=f32
    ).astype(bf16)
    width = couple.shape[0]

    piece = share // 2
    pairs = [
        (core * COLS + chip, (chip // 8) * COLS + 2 * (chip % 8) + core)
        for core in range(2)
        for chip in range(COLS)
    ]
    root_rows = lax.ppermute(
        lax.dynamic_slice_in_dim(root_right, row_id * piece, piece, 0), ("row", "col"), pairs
    )

    swap = [(0, 1), (1, 0)]
    other_sep = lax.ppermute(couple_sep, "row", swap)

    own = mul(inverse, right_side[0], precision=fine)
    first_low = lax.ppermute(own.astype(bf16), "row", [(0, 1)])
    total = sum_scatter(mul_t(lower, first_low).astype(bf16), "col", COLS)
    total = gather(total.astype(bf16), "col", COLS).reshape(PANEL, sources)
    solved = own - mul(inverse, total.astype(f32), precision=fine)

    updates = sum_scatter(mul(couple_sep, solved.astype(bf16)), ("row", "col"), COLS * 2)
    packed, _ = lax.optimization_barrier((packed, updates))
    off_half = packed[:, :half]
    diag_all = packed[:, half : half + 3].astype(f32).sum(1, keepdims=True)

    own_rows = (
        jnp.arange(SEPARATOR)[:, None] == (col_id * share + jnp.arange(share))[None, :]
    ).astype(bf16)
    wanted = jnp.concatenate([couple_sep, other_sep, own_rows], 1)
    mine = lax.dynamic_slice_in_dim(wanted, row_id * half, half, 0)
    part = mul(off_half, mine)
    sent = jnp.concatenate([part[:, width : 2 * width], part[:, :width], part[:, 2 * width :]], 1)
    inner = wanted * diag_all + part + lax.ppermute(sent.astype(bf16), "row", swap).astype(f32)
    outer = mul_t(off_half, inner.astype(bf16)) + lax.dynamic_slice_in_dim(
        diag_all * inner, row_id * half, half, 0
    )

    updates = gather(updates, "sub", SUBS).sum(0)
    rhs = gather(root_rows - updates, "col", COLS).reshape(half, sources)
    applied = mul_t(outer, rhs, precision=fine)
    theirs = lax.ppermute(applied[width:], "row", swap)
    value = solved - (applied[:width] + theirs[:width])
    root_part = applied[2 * width :] + theirs[width:]

    value = sum_scatter(mul_t(inverse, value, precision=fine), "col", COLS)
    later_low = gather(value.astype(bf16), "col", COLS).reshape(PANEL, sources)
    terms = lax.ppermute(mul(lower, later_low), "row", [(1, 0)])
    value = value - sum_scatter(mul_t(inverse, terms, precision=fine), "col", COLS)
    return value[None], root_part


def solution(mesh):
    return jax.shard_map(
        shards,
        mesh=mesh,
        in_specs=(
            P("sub", None, "col", "row"),
            P("sub", None, None),
            P("sub", ("row", "col"), None),
            P("sub", "row", "col", None),
            P("sub", None),
            P("col", None),
            P("sub", "row", None),
            P("col", None),
        ),
        out_specs=(P("sub", ("row", "col"), None), P("col", None)),
        check_vma=False,
    )
```

```python
import jax
import jax.numpy as jnp
from jax import lax
from jax.sharding import PartitionSpec as P

BLOCK = 256
PANEL = 2048
SEPARATOR = 1536
COLS = 16
SUBS = 8

f32 = jnp.float32
bf16 = jnp.bfloat16
fine = lax.Precision.HIGH
first_axes = (((0,), (0,)), ((), ()))


def mul(left, right, **kw):
    return jnp.dot(left, right, preferred_element_type=f32, **kw)


def mul_t(left, right, **kw):
    return lax.dot_general(left, right, first_axes, preferred_element_type=f32, **kw)


def split3(value):
    pieces = []
    for _ in range(3):
        pieces.append(lax.reduce_precision(value, 8, 7))
        value = value - pieces[-1]
    return pieces


def plane(step_y, step_x, source=1, target=1):
    return [
        (
            source * COLS + 4 * y + x,
            target * COLS + 4 * ((y + step_y) % 4) + (x + step_x) % 4,
        )
        for y in range(4)
        for x in range(4)
    ]


def send(value, pairs):
    return lax.ppermute(value, ("row", "col"), pairs)


def sum_scatter(partial, axes, count):
    parts = partial.reshape(count, -1, partial.shape[-1])
    here = lax.axis_index(axes)
    own = lax.dynamic_index_in_dim(parts, here, 0)
    others = lax.all_to_all(parts.astype(bf16), axes, 0, 0).astype(f32)
    index = lax.broadcasted_iota(jnp.int32, (count, 1, 1), 0)
    return jnp.where(index == here, own, others).sum(0)


def gather(chunk, axes, count):
    spread = jnp.broadcast_to(chunk[None], (count,) + chunk.shape)
    return lax.all_to_all(spread, axes, 0, 0)


def shards(
    factor_cols,
    block_pattern,
    diag_inverse,
    coupling_cols,
    separator_rows,
    root_inverse,
    right_side,
    root_right,
):
    table = block_pattern[0]
    inverse = diag_inverse[0]
    couple = coupling_cols[0, 0]
    rows_sep = separator_rows[0]
    row_id = lax.axis_index("row")
    col_id = lax.axis_index("col")
    sources = right_side.shape[-1]

    own = mul(inverse, right_side[0], precision=fine)
    own_low = own.astype(bf16)

    blocks = lax.dynamic_slice(table, (PANEL // BLOCK, col_id // 2), (PANEL // BLOCK, 1))
    lower = factor_cols[0, 0] * jnp.repeat(blocks[:, 0], BLOCK)[None, :].astype(bf16)
    width = lower.shape[0]
    square = lax.dynamic_slice_in_dim(inverse, col_id * width, width, 1)
    line = lax.broadcasted_iota(jnp.int32, inverse.shape, 0) + col_id * width
    apart = jnp.where(lax.broadcasted_iota(jnp.int32, inverse.shape, 1) == line, 0.0, inverse)
    diag = jnp.where(jnp.eye(width, dtype=bool), square, 0.0).sum(0, keepdims=True)
    rest = jnp.concatenate(split3(diag) + [jnp.zeros((13, width), f32)], 0)
    rest = jnp.pad(rest, ((0, 0), (0, PANEL - width)))
    apart = jnp.concatenate([apart, rest], 0).astype(bf16)
    lowers = jnp.concatenate([lower] + [send(lower, plane(-k, 0)) for k in (1, 2, 3)], 0)
    first = jnp.concatenate([send(own_low, plane(-k, 0, 0, 1)) for k in range(4)], 0)
    aparts = [apart] + [send(apart, plane(0, -k)) for k in (1, 2, 3)]
    elim = []
    for k in range(4):
        chip = col_id // 4 * 4 + (col_id + k) % 4
        rows = lax.dynamic_slice_in_dim(lowers, chip * width, width, 1).astype(f32)
        scale = aparts[k][width : width + 3, :width].astype(f32).sum(0, keepdims=True)
        off = lax.dot_general(
            lowers, aparts[k][:width], (((1,), (1,)), ((), ())), preferred_element_type=f32
        )
        elim.append(off + rows * scale)
    elim = jnp.concatenate(elim, 1)
    terms = mul_t(elim, first.astype(f32), precision=fine)
    solved = own - terms[:width]
    for k in (1, 2, 3):
        solved = solved - send(terms[k * width : (k + 1) * width], plane(0, k))

    share = root_inverse.shape[0]
    half = SEPARATOR // 2
    lane = lax.broadcasted_iota(jnp.int32, root_inverse.shape, 1)
    line = lax.broadcasted_iota(jnp.int32, root_inverse.shape, 0) + col_id * share
    on_diag = lane == line
    diag = jnp.where(on_diag, root_inverse, 0.0).sum(1, keepdims=True)
    pieces = split3(diag)
    off = lax.dynamic_slice_in_dim(jnp.where(on_diag, 0.0, root_inverse), row_id * half, half, 1)
    packed = jnp.concatenate([off] + pieces + [jnp.zeros((share, 125), f32)], 1).astype(bf16)
    packed, _ = lax.optimization_barrier((packed, lowers))
    for step_y, step_x, place in ((0, 1, col_id % 4), (1, 0, col_id // 4)):
        whole = jnp.zeros((4,) + packed.shape, bf16)
        for k in range(4):
            pairs = [(i % COLS, j % COLS) for i, j in plane(-k * step_y, -k * step_x)]
            piece = lax.ppermute(packed, "col", pairs) if k else packed
            whole = lax.dynamic_update_slice_in_dim(whole, piece[None], (place + k) % 4, 0)
        packed = whole
    packed = packed.reshape(SEPARATOR, half + 128)

    onehot = (jnp.arange(SEPARATOR)[:, None] == rows_sep[None, :]).astype(bf16)
    couple_sep = lax.dot_general(
        onehot, couple, (((1,), (1,)), ((), ())), preferred_element_type=f32
    ).astype(bf16)

    piece = share // 2
    pairs = [
        (core * COLS + chip, (chip // 8) * COLS + 2 * (chip % 8) + core)
        for core in range(2)
        for chip in range(COLS)
    ]
    root_rows = lax.ppermute(
        lax.dynamic_slice_in_dim(root_right, row_id * piece, piece, 0), ("row", "col"), pairs
    )

    swap = [(0, 1), (1, 0)]
    other_sep = lax.ppermute(couple_sep, "row", swap)

    updates = sum_scatter(mul(couple_sep, solved.astype(bf16)), ("row", "col"), COLS * 2)
    packed, _ = lax.optimization_barrier((packed, updates))
    off_half = packed[:, :half]
    diag_all = packed[:, half : half + 3].astype(f32).sum(1, keepdims=True)

    own_rows = (
        jnp.arange(SEPARATOR)[:, None] == (col_id * share + jnp.arange(share))[None, :]
    ).astype(bf16)
    wanted = jnp.concatenate([couple_sep, other_sep, own_rows], 1)
    mine = lax.dynamic_slice_in_dim(wanted, row_id * half, half, 0)
    part = mul(off_half, mine)
    sent = jnp.concatenate([part[:, width : 2 * width], part[:, :width], part[:, 2 * width :]], 1)
    inner = wanted * diag_all + part + lax.ppermute(sent.astype(bf16), "row", swap).astype(f32)
    outer = mul_t(off_half, inner.astype(bf16)) + lax.dynamic_slice_in_dim(
        diag_all * inner, row_id * half, half, 0
    )

    updates = gather(updates, "sub", SUBS).sum(0)
    rhs = gather(root_rows - updates, "col", COLS).reshape(half, sources)
    applied = mul_t(outer, rhs, precision=fine)
    theirs = lax.ppermute(applied[width:], "row", swap)
    value = solved - (applied[:width] + theirs[:width])
    root_part = applied[2 * width :] + theirs[width:]

    later = jnp.concatenate([value] + [send(value, plane(0, -k)) for k in (1, 2, 3)], 0)
    terms = mul(elim, later, precision=fine)
    taken = terms[:width]
    for k in (1, 2, 3):
        taken = taken + send(terms[k * width : (k + 1) * width], plane(k, 0))
    value = value - lax.ppermute(taken, "row", [(1, 0)])
    value = sum_scatter(mul_t(inverse, value, precision=fine), "col", COLS)
    return value[None], root_part


def solution(mesh):
    return jax.shard_map(
        shards,
        mesh=mesh,
        in_specs=(
            P("sub", None, "col", "row"),
            P("sub", None, None),
            P("sub", ("row", "col"), None),
            P("sub", "row", "col", None),
            P("sub", None),
            P("col", None),
            P("sub", "row", None),
            P("col", None),
        ),
        out_specs=(P("sub", ("row", "col"), None), P("col", None)),
        check_vma=False,
    )
```

```python
import jax
import jax.numpy as jnp
from jax import lax
from jax.sharding import PartitionSpec as P

BLOCK = 256
PANEL = 2048
SEPARATOR = 1536
COLS = 16
SUBS = 8

f32 = jnp.float32
bf16 = jnp.bfloat16
fine = lax.Precision.HIGH
first_axes = (((0,), (0,)), ((), ()))


def mul(left, right, **kw):
    return jnp.dot(left, right, preferred_element_type=f32, **kw)


def mul_t(left, right, **kw):
    return lax.dot_general(left, right, first_axes, preferred_element_type=f32, **kw)


def split3(value):
    pieces = []
    for _ in range(3):
        pieces.append(lax.reduce_precision(value, 8, 7))
        value = value - pieces[-1]
    return pieces


def after(value, other):
    return lax.optimization_barrier((value, other))[0]


def plane(step_y, step_x):
    return [
        (4 * y + x, 4 * ((y + step_y) % 4) + (x + step_x) % 4) for y in range(4) for x in range(4)
    ]


def sum_scatter(partial, axes, count):
    parts = partial.reshape(count, -1, partial.shape[-1])
    here = lax.axis_index(axes)
    own = lax.dynamic_index_in_dim(parts, here, 0)
    others = lax.all_to_all(parts.astype(bf16), axes, 0, 0).astype(f32)
    index = lax.broadcasted_iota(jnp.int32, (count, 1, 1), 0)
    return jnp.where(index == here, own, others).sum(0)


def gather(chunk, axes, count):
    spread = jnp.broadcast_to(chunk[None], (count,) + chunk.shape)
    return lax.all_to_all(spread, axes, 0, 0)


def shards(
    factor_cols,
    block_pattern,
    diag_inverse,
    coupling_cols,
    separator_rows,
    root_inverse,
    right_side,
    root_right,
):
    table = block_pattern[0]
    inverse = diag_inverse[0]
    couple = coupling_cols[0, 0]
    rows_sep = separator_rows[0]
    row_id = lax.axis_index("row")
    col_id = lax.axis_index("col")
    sources = right_side.shape[-1]
    col_y, col_x = col_id // 4, col_id % 4

    blocks = lax.dynamic_slice(table, (PANEL // BLOCK, col_id // 2), (PANEL // BLOCK, 1))
    lower = factor_cols[0, 0] * jnp.repeat(blocks[:, 0], BLOCK)[None, :].astype(bf16)
    width = lower.shape[0]

    own = mul(inverse, right_side[0], precision=fine)
    first_low = lax.ppermute(own.astype(bf16), "row", [(0, 1)])
    partial = mul_t(lower, first_low).astype(bf16)
    total = lax.all_to_all(partial.reshape(COLS, width, sources), "col", 0, 0)
    total = total.astype(f32).sum(0).astype(bf16)
    solved = own - mul(inverse, gather(total, "col", COLS).reshape(PANEL, sources).astype(f32), precision=fine)

    share = root_inverse.shape[0]
    half = SEPARATOR // 2
    root_inverse = after(root_inverse, partial)
    lane = lax.broadcasted_iota(jnp.int32, root_inverse.shape, 1)
    line = lax.broadcasted_iota(jnp.int32, root_inverse.shape, 0) + col_id * share
    on_diag = lane == line
    diag = jnp.where(on_diag, root_inverse, 0.0).sum(1, keepdims=True)
    pieces = split3(diag)
    off = lax.dynamic_slice_in_dim(jnp.where(on_diag, 0.0, root_inverse), row_id * half, half, 1)
    packed = jnp.concatenate([off] + pieces + [jnp.zeros((share, 125), f32)], 1).astype(bf16)
    for step_y, step_x, place, dep in ((0, 1, col_x, partial), (1, 0, col_y, total)):
        packed = after(packed, dep)
        whole = jnp.zeros((4,) + packed.shape, bf16)
        for k in range(4):
            piece = lax.ppermute(packed, "col", plane(-k * step_y, -k * step_x)) if k else packed
            whole = lax.dynamic_update_slice_in_dim(whole, piece[None], (place + k) % 4, 0)
        packed = whole
    packed = packed.reshape(SEPARATOR, half + 128)

    onehot = (jnp.arange(SEPARATOR)[:, None] == rows_sep[None, :]).astype(bf16)
    couple_sep = lax.dot_general(
        onehot, couple, (((1,), (1,)), ((), ())), preferred_element_type=f32
    ).astype(bf16)

    piece = share // 2
    pairs = [
        (core * COLS + chip, (chip // 8) * COLS + 2 * (chip % 8) + core)
        for core in range(2)
        for chip in range(COLS)
    ]
    root_rows = lax.ppermute(
        lax.dynamic_slice_in_dim(root_right, row_id * piece, piece, 0), ("row", "col"), pairs
    )

    swap = [(0, 1), (1, 0)]
    other_sep = lax.ppermute(couple_sep, "row", swap)

    updates = mul(couple_sep, solved.astype(bf16)).astype(bf16).reshape(COLS * 2, -1, sources)
    updates = lax.all_to_all(updates, ("row", "col"), 0, 0).astype(f32).sum(0)
    updates = gather(updates, "sub", SUBS).sum(0)
    rhs = gather(root_rows - updates, "col", COLS).reshape(half, sources)

    packed = after(packed, updates)
    off_half = packed[:, :half]
    diag_all = packed[:, half : half + 3].astype(f32).sum(1, keepdims=True)

    own_rows = (
        jnp.arange(SEPARATOR)[:, None] == (col_id * share + jnp.arange(share))[None, :]
    ).astype(bf16)
    wanted = jnp.concatenate([couple_sep, other_sep, own_rows], 1)
    mine = lax.dynamic_slice_in_dim(wanted, row_id * half, half, 0)
    part = mul(off_half, mine)
    sent = jnp.concatenate([part[:, width : 2 * width], part[:, :width], part[:, 2 * width :]], 1)
    inner = wanted * diag_all + part + lax.ppermute(sent.astype(bf16), "row", swap).astype(f32)
    outer = mul_t(off_half, inner.astype(bf16)) + lax.dynamic_slice_in_dim(
        diag_all * inner, row_id * half, half, 0
    )

    applied = mul_t(outer, rhs, precision=fine)
    theirs = lax.ppermute(applied[width:], "row", swap)
    value = solved - (applied[:width] + theirs[:width])
    root_part = applied[2 * width :] + theirs[width:]

    value = sum_scatter(mul_t(inverse, value, precision=fine), "col", COLS)
    later_low = gather(value.astype(bf16), "col", COLS).reshape(PANEL, sources)
    terms = lax.ppermute(mul(lower, later_low), "row", [(1, 0)])
    value = value - sum_scatter(mul_t(inverse, terms, precision=fine), "col", COLS)
    return value[None], root_part


def solution(mesh):
    return jax.shard_map(
        shards,
        mesh=mesh,
        in_specs=(
            P("sub", None, "col", "row"),
            P("sub", None, None),
            P("sub", ("row", "col"), None),
            P("sub", "row", "col", None),
            P("sub", None),
            P("col", None),
            P("sub", "row", None),
            P("col", None),
        ),
        out_specs=(P("sub", ("row", "col"), None), P("col", None)),
        check_vma=False,
    )
```

```python
import jax
import jax.numpy as jnp
from jax import lax
from jax.sharding import PartitionSpec as P

BLOCK = 256
PANEL = 2048
SEPARATOR = 1536
COLS = 16
SUBS = 8

f32 = jnp.float32
bf16 = jnp.bfloat16
fine = lax.Precision.HIGH
first_axes = (((0,), (0,)), ((), ()))


def mul(left, right, **kw):
    return jnp.dot(left, right, preferred_element_type=f32, **kw)


def mul_t(left, right, **kw):
    return lax.dot_general(left, right, first_axes, preferred_element_type=f32, **kw)


def after(value, other):
    return lax.optimization_barrier((value, other))[0]


def sum_scatter(partial, axes, count):
    parts = partial.reshape(count, -1, partial.shape[-1])
    here = lax.axis_index(axes)
    own = lax.dynamic_index_in_dim(parts, here, 0)
    others = lax.all_to_all(parts.astype(bf16), axes, 0, 0).astype(f32)
    index = lax.broadcasted_iota(jnp.int32, (count, 1, 1), 0)
    return jnp.where(index == here, own, others).sum(0)


def gather(chunk, axes, count):
    spread = jnp.broadcast_to(chunk[None], (count,) + chunk.shape)
    return lax.all_to_all(spread, axes, 0, 0)


def shards(
    factor_cols,
    block_pattern,
    diag_inverse,
    coupling_cols,
    separator_rows,
    root_inverse,
    right_side,
    root_right,
):
    table = block_pattern[0]
    inverse = diag_inverse[0]
    couple = coupling_cols[0, 0]
    rows_sep = separator_rows[0]
    row_id = lax.axis_index("row")
    col_id = lax.axis_index("col")
    sources = right_side.shape[-1]
    band_id = lax.axis_index(("sub", "row"))

    blocks = lax.dynamic_slice(table, (PANEL // BLOCK, col_id // 2), (PANEL // BLOCK, 1))
    lower = factor_cols[0, 0] * jnp.repeat(blocks[:, 0], BLOCK)[None, :].astype(bf16)
    width = lower.shape[0]

    own = mul(inverse, right_side[0], precision=fine)
    first_low = lax.ppermute(own.astype(bf16), "row", [(0, 1)])
    partial = mul_t(lower, first_low).astype(bf16)
    total = lax.all_to_all(partial.reshape(COLS, width, sources), "col", 0, 0)
    total = total.astype(f32).sum(0).astype(bf16)

    share = root_inverse.shape[0]
    band = SEPARATOR // (2 * SUBS)
    root_inverse = after(root_inverse, partial)
    gram = mul_t(
        root_inverse,
        lax.dynamic_slice_in_dim(root_inverse, band_id * band, band, 1),
        precision=fine,
    ).reshape(COLS, share, band)
    own_gram = lax.dynamic_index_in_dim(gram, col_id, 0)
    gram = jnp.pad(gram.astype(bf16), ((0, 0), (0, 0), (0, sources - band)))

    both = jnp.concatenate([jnp.broadcast_to(total[None], (COLS,) + total.shape), gram], 1)
    both = lax.all_to_all(both, "col", 0, 0)
    total = both[:, :width].reshape(PANEL, sources)
    solved = own - mul(inverse, total.astype(f32), precision=fine)
    chips = lax.broadcasted_iota(jnp.int32, (COLS, 1, 1), 0)
    gram = jnp.where(chips == col_id, own_gram, both[:, width:, :band].astype(f32)).sum(0)

    onehot = (jnp.arange(SEPARATOR)[:, None] == rows_sep[None, :]).astype(bf16)
    couple_sep = lax.dot_general(
        onehot, couple, (((1,), (1,)), ((), ())), preferred_element_type=f32
    ).astype(bf16)

    updates = mul(couple_sep, solved.astype(bf16)).astype(bf16).reshape(2 * SUBS, band, sources)
    updates = lax.all_to_all(updates, ("sub", "row"), 0, 0).astype(f32).sum(0)
    here = (band_id == col_id).astype(f32)
    rhs = gather(here * root_right - updates, "col", COLS).sum(0)
    applied = mul(gram, rhs, precision=fine)
    half = share // 2
    kept = lax.dynamic_slice_in_dim(applied, row_id * half, half, 0)
    sent = lax.dynamic_slice_in_dim(applied, (1 - row_id) * half, half, 0)
    swap = [(0, 1), (1, 0)]
    kept = gather(kept + lax.ppermute(sent, "row", swap), "sub", SUBS).sum(0)
    other = lax.ppermute(kept, "row", swap)
    root_part = jnp.where(
        row_id == 0, jnp.concatenate([kept, other], 0), jnp.concatenate([other, kept], 0)
    )
    root_full = gather(root_part.astype(bf16), "col", COLS).reshape(SEPARATOR, sources)
    value = solved - mul_t(couple_sep, root_full)

    value = sum_scatter(mul_t(inverse, value, precision=fine), "col", COLS)
    later_low = gather(value.astype(bf16), "col", COLS).reshape(PANEL, sources)
    terms = lax.ppermute(mul(lower, later_low), "row", [(1, 0)])
    value = value - sum_scatter(mul_t(inverse, terms, precision=fine), "col", COLS)
    return value[None], root_part


def solution(mesh):
    return jax.shard_map(
        shards,
        mesh=mesh,
        in_specs=(
            P("sub", None, "col", "row"),
            P("sub", None, None),
            P("sub", ("row", "col"), None),
            P("sub", "row", "col", None),
            P("sub", None),
            P("col", None),
            P("sub", "row", None),
            P("col", None),
        ),
        out_specs=(P("sub", ("row", "col"), None), P("col", None)),
        check_vma=False,
    )
```

```python
import jax
import jax.numpy as jnp
from jax import lax
from jax.sharding import PartitionSpec as P

BLOCK = 256
PANEL = 2048
SEPARATOR = 1536
COLS = 16
SUBS = 8

f32 = jnp.float32
bf16 = jnp.bfloat16
fine = lax.Precision.HIGH
along_x = [[4 * y + x for x in range(4)] for y in range(4)]
along_y = [[4 * y + x for y in range(4)] for x in range(4)]
first_axes = (((0,), (0,)), ((), ()))


def mul(left, right, **kw):
    return jnp.dot(left, right, preferred_element_type=f32, **kw)


def mul_t(left, right, **kw):
    return lax.dot_general(left, right, first_axes, preferred_element_type=f32, **kw)


def after(value, other):
    return lax.optimization_barrier((value, other))[0]


def send(value, step_y, step_x):
    pairs = [
        (COLS + 4 * y + x, COLS + 4 * ((y + step_y) % 4) + (x + step_x) % 4)
        for y in range(4)
        for x in range(4)
    ]
    return lax.ppermute(value, ("row", "col"), pairs)


def twice(product, low, value):
    high = lax.reduce_precision(value, 8, 7)
    return product(low, high.astype(bf16)) + product(low, (value - high).astype(bf16))


def sum_scatter(partial, axes, count):
    parts = partial.reshape(count, -1, partial.shape[-1])
    here = lax.axis_index(axes)
    own = lax.dynamic_index_in_dim(parts, here, 0)
    others = lax.all_to_all(parts.astype(bf16), axes, 0, 0).astype(f32)
    index = lax.broadcasted_iota(jnp.int32, (count, 1, 1), 0)
    return jnp.where(index == here, own, others).sum(0)


def gather(chunk, axes, count):
    spread = jnp.broadcast_to(chunk[None], (count,) + chunk.shape)
    return lax.all_to_all(spread, axes, 0, 0)


def shards(
    factor_cols,
    block_pattern,
    diag_inverse,
    coupling_cols,
    separator_rows,
    root_inverse,
    right_side,
    root_right,
):
    table = block_pattern[0]
    inverse = diag_inverse[0]
    couple = coupling_cols[0, 0]
    rows_sep = separator_rows[0]
    row_id = lax.axis_index("row")
    col_id = lax.axis_index("col")
    sources = right_side.shape[-1]
    col_y, col_x = col_id // 4, col_id % 4
    band_id = lax.axis_index(("row", "sub"))

    blocks = lax.dynamic_slice(table, (PANEL // BLOCK, col_id // 2), (PANEL // BLOCK, 1))
    lower = factor_cols[0, 0] * jnp.repeat(blocks[:, 0], BLOCK)[None, :].astype(bf16)
    width = lower.shape[0]

    own = mul(inverse, right_side[0], precision=fine)
    first_low = lax.ppermute(own.astype(bf16), "row", [(0, 1)])
    partial = mul_t(lower, first_low).astype(bf16)
    total = lax.all_to_all(partial.reshape(COLS, width, sources), "col", 0, 0)
    total = total.astype(f32).sum(0).astype(bf16)

    share = root_inverse.shape[0]
    band = SEPARATOR // (2 * SUBS)
    root_inverse = after(root_inverse, partial)
    gram = mul_t(
        root_inverse,
        lax.dynamic_slice_in_dim(root_inverse, band_id * band, band, 1),
        precision=fine,
    ).reshape(COLS, share, band)
    own_gram = lax.dynamic_index_in_dim(gram, col_id, 0)
    gram = jnp.pad(gram.astype(bf16), ((0, 0), (0, 0), (0, sources - band)))

    both = jnp.concatenate([jnp.broadcast_to(total[None], (COLS,) + total.shape), gram], 1)
    both = lax.all_to_all(both, "col", 0, 0)
    total = both[:, :width].reshape(PANEL, sources)
    solved = own - mul(inverse, total.astype(f32), precision=fine)
    chips = lax.broadcasted_iota(jnp.int32, (COLS, 1, 1), 0)
    gram = jnp.where(chips == col_id, own_gram, both[:, width:, :band].astype(f32)).sum(0)

    flipped = lax.optimization_barrier(after(inverse, partial).T)
    flipped_own = lax.dynamic_slice_in_dim(flipped, col_id * width, width, 0)
    onehot = (jnp.arange(SEPARATOR)[:, None] == rows_sep[None, :]).astype(bf16)
    couple_sep = lax.dot_general(
        onehot, couple, (((1,), (1,)), ((), ())), preferred_element_type=f32
    ).astype(bf16)

    swap = [(0, 1), (1, 0)]
    updates = mul(couple_sep, solved.astype(bf16)).reshape(2, SUBS * band, sources)
    sent = lax.dynamic_index_in_dim(updates, 1 - row_id, 0, False)
    updates = lax.dynamic_index_in_dim(updates, row_id, 0, False)
    updates = sum_scatter(updates + lax.ppermute(sent, "row", swap), "sub", SUBS)
    here = (band_id == col_id).astype(f32)
    rhs = gather(here * root_right - updates, "col", COLS).sum(0)
    panels = [after(inverse, total).astype(bf16)]
    panels = jnp.concatenate(panels + [send(panels[0], 0, -k) for k in (1, 2, 3)], 0)
    rhs = after(rhs, panels)
    lowers = [after(lower, updates)]
    lowers = jnp.concatenate(lowers + [send(lowers[0], -k, 0) for k in (1, 2, 3)], 0)
    applied = mul(gram, rhs, precision=fine)
    half = share // 2
    kept = lax.dynamic_slice_in_dim(applied, row_id * half, half, 0)
    sent = lax.dynamic_slice_in_dim(applied, (1 - row_id) * half, half, 0)
    kept = gather(kept + lax.ppermute(sent, "row", swap), "sub", SUBS).sum(0)
    other = lax.ppermute(kept, "row", swap)
    root_part = jnp.where(
        row_id == 0, jnp.concatenate([kept, other], 0), jnp.concatenate([other, kept], 0)
    )
    root_full = gather(root_part.astype(bf16), "col", COLS).reshape(SEPARATOR, sources)
    value = solved - mul_t(couple_sep, after(root_full, lowers))

    later = lax.all_to_all(
        jnp.broadcast_to(value[None], (4,) + value.shape), "col", 0, 0, axis_index_groups=along_x
    )
    later = [lax.dynamic_index_in_dim(later, (col_x + k) % 4, 0, False) for k in range(4)]
    later = twice(mul_t, panels, jnp.concatenate(later, 0))
    terms = twice(mul, lowers, later).reshape(4, width, sources)
    chips = lax.broadcasted_iota(jnp.int32, (4, 1, 1), 0)
    terms = sum(jnp.where(chips == (col_y + k) % 4, terms[k], 0.0) for k in range(4))
    taken = lax.all_to_all(terms, "col", 0, 0, axis_index_groups=along_y).sum(0)
    value = value - lax.ppermute(taken, "row", [(1, 0)])

    shares = mul(flipped, value, precision=fine).astype(bf16).reshape(COLS, width, sources)
    shares = lax.all_to_all(shares, "col", 0, 0).astype(f32)
    chips = lax.broadcasted_iota(jnp.int32, (COLS, 1, 1), 0)
    value = jnp.where(chips == col_id, mul(flipped_own, value, precision=fine), shares).sum(0)
    return value[None], root_part


def solution(mesh):
    return jax.shard_map(
        shards,
        mesh=mesh,
        in_specs=(
            P("sub", None, "col", "row"),
            P("sub", None, None),
            P("sub", ("row", "col"), None),
            P("sub", "row", "col", None),
            P("sub", None),
            P("col", None),
            P("sub", "row", None),
            P("col", None),
        ),
        out_specs=(P("sub", ("row", "col"), None), P("col", None)),
        check_vma=False,
    )
```

```python
import jax
import jax.numpy as jnp
from jax import lax
from jax.sharding import PartitionSpec as P

BLOCK = 256
PANEL = 2048
SEPARATOR = 1536
COLS = 16
SUBS = 8

f32 = jnp.float32
bf16 = jnp.bfloat16
fine = lax.Precision.HIGH
first_axes = (((0,), (0,)), ((), ()))


def mul(left, right, **kw):
    return jnp.dot(left, right, preferred_element_type=f32, **kw)


def mul_t(left, right, **kw):
    return lax.dot_general(left, right, first_axes, preferred_element_type=f32, **kw)


def after(value, other):
    return lax.optimization_barrier((value, other))[0]


def sum_scatter(partial, axes, count):
    parts = partial.reshape(count, -1, partial.shape[-1])
    return lax.all_to_all(parts, axes, 0, 0).astype(f32).sum(0)


def gather(chunk, axes, count):
    spread = jnp.broadcast_to(chunk[None], (count,) + chunk.shape)
    return lax.all_to_all(spread, axes, 0, 0)


def shards(
    factor_cols,
    block_pattern,
    diag_inverse,
    coupling_cols,
    separator_rows,
    root_inverse,
    right_side,
    root_right,
):
    table = block_pattern[0]
    inverse = diag_inverse[0]
    couple = coupling_cols[0, 0]
    rows_sep = separator_rows[0]
    row_id = lax.axis_index("row")
    col_id = lax.axis_index("col")
    sources = right_side.shape[-1]
    factor = factor_cols[0, 0]
    width = factor.shape[0]
    half = PANEL // 2
    swap = [(0, 1), (1, 0)]
    up, down = [(0, 1)], [(1, 0)]
    on_first = row_id == 0

    count = half // BLOCK
    blocks = lax.dynamic_slice(
        table, (PANEL // BLOCK + row_id * count, col_id // 2), (count, 1)
    )
    lower = jnp.where(on_first, lax.ppermute(factor[:, :half], "row", down), factor[:, half:])
    lower = lower * jnp.repeat(blocks[:, 0], BLOCK)[None, :].astype(bf16)

    own = mul(inverse, right_side[0], precision=fine)
    low = own.astype(bf16)
    low = jnp.where(on_first, low, lax.ppermute(low, "row", up))
    partial = mul_t(lower, low).astype(bf16)
    total = sum_scatter(partial, "col", COLS).astype(bf16)

    flipped = lax.optimization_barrier(after(inverse, partial).T)
    flipped_own = lax.dynamic_slice_in_dim(flipped, col_id * width, width, 0)
    flipped_half = jnp.where(
        on_first, lax.ppermute(flipped[:half], "row", down), flipped[half:]
    )
    onehot = (jnp.arange(SEPARATOR)[:, None] == after(rows_sep, partial)[None, :]).astype(bf16)
    couple_sep = lax.dot_general(
        onehot, couple, (((1,), (1,)), ((), ())), preferred_element_type=f32
    ).astype(bf16)
    rows = SEPARATOR // (2 * COLS)
    pairs = [
        (core * COLS + chip, (chip // 8) * COLS + 2 * (chip % 8) + core)
        for core in range(2)
        for chip in range(COLS)
    ]
    root_rows = lax.dynamic_slice_in_dim(after(root_right, partial), row_id * rows, rows, 0)
    root_rows = lax.ppermute(root_rows, ("row", "col"), pairs)
    sep_half = SEPARATOR // 2
    root_half = lax.dynamic_slice_in_dim(after(root_inverse, partial), row_id * sep_half, sep_half, 1)

    total = gather(total, "col", COLS).reshape(half, sources).astype(f32)
    terms = mul_t(flipped_half, total, precision=fine)
    solved = own - jnp.where(on_first, 0.0, terms) - lax.ppermute(terms, "row", up)

    updates = sum_scatter(
        mul(couple_sep, solved.astype(bf16)).astype(bf16), ("row", "col"), COLS * 2
    )
    updates = gather(updates, "sub", SUBS).sum(0)
    rhs = gather(root_rows - updates, "col", COLS).reshape(sep_half, sources)
    inner = mul(root_half, rhs, precision=fine)
    inner = inner + lax.ppermute(inner, "row", swap)
    root_rows = sum_scatter(mul_t(root_half, inner, precision=fine), "col", COLS)
    root_low = gather(root_rows.astype(bf16), "col", COLS).reshape(sep_half, sources)
    other_low = lax.ppermute(root_low, "row", swap)
    mine = lax.dynamic_slice_in_dim(couple_sep, row_id * sep_half, sep_half, 0)
    others = lax.dynamic_slice_in_dim(couple_sep, (1 - row_id) * sep_half, sep_half, 0)
    value = solved - mul_t(mine, root_low) - mul_t(others, other_low)

    later = jnp.where(on_first, lax.ppermute(value, "row", down), value)
    later = sum_scatter(mul(flipped_half, later, precision=fine), "col", COLS).astype(bf16)
    later = gather(later, "col", COLS).reshape(half, sources)
    terms = mul(lower, later)
    value = value - jnp.where(on_first, terms, 0.0) - lax.ppermute(terms, "row", down)

    shares = mul(flipped, value, precision=fine).astype(bf16).reshape(COLS, width, sources)
    shares = lax.all_to_all(shares, "col", 0, 0).astype(f32)
    chips = lax.broadcasted_iota(jnp.int32, (COLS, 1, 1), 0)
    value = jnp.where(chips == col_id, mul(flipped_own, value, precision=fine), shares).sum(0)

    root_rows = lax.ppermute(root_rows, ("row", "col"), [(j, i) for i, j in pairs])
    theirs = lax.ppermute(root_rows, "row", swap)
    root_part = jnp.where(
        on_first,
        jnp.concatenate([root_rows, theirs], 0),
        jnp.concatenate([theirs, root_rows], 0),
    )
    return value[None], root_part


def solution(mesh):
    return jax.shard_map(
        shards,
        mesh=mesh,
        in_specs=(
            P("sub", None, "col", "row"),
            P("sub", None, None),
            P("sub", ("row", "col"), None),
            P("sub", "row", "col", None),
            P("sub", None),
            P("col", None),
            P("sub", "row", None),
            P("col", None),
        ),
        out_specs=(P("sub", ("row", "col"), None), P("col", None)),
        check_vma=False,
    )
```

```python
import jax
import jax.numpy as jnp
from jax import lax
from jax.sharding import PartitionSpec as P

BLOCK = 256
PANEL = 2048
SEPARATOR = 1536
COLS = 16
SUBS = 8

f32 = jnp.float32
bf16 = jnp.bfloat16
fine = lax.Precision.HIGH
first_axes = (((0,), (0,)), ((), ()))


def mul(left, right, **kw):
    return jnp.dot(left, right, preferred_element_type=f32, **kw)


def mul_t(left, right, **kw):
    return lax.dot_general(left, right, first_axes, preferred_element_type=f32, **kw)


def after(value, other):
    return lax.optimization_barrier((value, other))[0]


def sum_scatter(partial, axes, count):
    parts = partial.reshape(count, -1, partial.shape[-1])
    here = lax.axis_index(axes)
    own = lax.dynamic_index_in_dim(parts, here, 0)
    others = lax.all_to_all(parts.astype(bf16), axes, 0, 0).astype(f32)
    index = lax.broadcasted_iota(jnp.int32, (count, 1, 1), 0)
    return jnp.where(index == here, own, others).sum(0)


def gather(chunk, axes, count):
    spread = jnp.broadcast_to(chunk[None], (count,) + chunk.shape)
    return lax.all_to_all(spread, axes, 0, 0)


def shards(
    factor_cols,
    block_pattern,
    diag_inverse,
    coupling_cols,
    separator_rows,
    root_inverse,
    right_side,
    root_right,
):
    table = block_pattern[0]
    inverse = diag_inverse[0]
    couple = coupling_cols[0, 0]
    rows_sep = separator_rows[0]
    row_id = lax.axis_index("row")
    col_id = lax.axis_index("col")
    sources = right_side.shape[-1]
    sub_id = lax.axis_index("sub")

    blocks = lax.dynamic_slice(table, (PANEL // BLOCK, col_id // 2), (PANEL // BLOCK, 1))
    lower = factor_cols[0, 0] * jnp.repeat(blocks[:, 0], BLOCK)[None, :].astype(bf16)
    width = lower.shape[0]

    own = mul(inverse, right_side[0], precision=fine)
    first_low = lax.ppermute(own.astype(bf16), "row", [(0, 1)])
    partial = mul_t(lower, first_low).astype(bf16)
    total = lax.all_to_all(partial.reshape(COLS, width, sources), "col", 0, 0)
    total = total.astype(f32).sum(0).astype(bf16)

    share = root_inverse.shape[0]
    chunk = share // 2
    half = SEPARATOR // 2
    root_inverse = after(root_inverse, partial)
    rows_half = lax.dynamic_slice_in_dim(root_inverse, row_id * half, half, 1)
    gram = [
        mul_t(
            rows_half,
            lax.dynamic_slice_in_dim(root_inverse, (2 * sub_id + k) * share, share, 1),
            precision=fine,
        ).reshape(COLS, chunk, share)
        for k in range(2)
    ]
    gram = jnp.concatenate(gram, 1)
    own_gram = lax.dynamic_index_in_dim(gram, col_id, 0)
    gram = jnp.pad(gram.astype(bf16), ((0, 0), (0, 0), (0, sources - share)))

    both = jnp.concatenate([jnp.broadcast_to(total[None], (COLS,) + total.shape), gram], 1)
    both = lax.all_to_all(both, "col", 0, 0)
    total = both[:, :width].reshape(PANEL, sources)
    solved = own - mul(inverse, total.astype(f32), precision=fine)
    chips = lax.broadcasted_iota(jnp.int32, (COLS, 1, 1), 0)
    gram = jnp.where(chips == col_id, own_gram, both[:, width:, :share].astype(f32)).sum(0)

    onehot = (jnp.arange(SEPARATOR)[:, None] == rows_sep[None, :]).astype(bf16)
    couple_sep = lax.dot_general(
        onehot, couple, (((1,), (1,)), ((), ())), preferred_element_type=f32
    ).astype(bf16)

    swap = [(0, 1), (1, 0)]
    pairs = [
        (core * COLS + chip, (chip // 8) * COLS + 2 * (chip % 8) + core)
        for core in range(2)
        for chip in range(COLS)
    ]
    root_rows = lax.dynamic_slice_in_dim(after(root_right, partial), row_id * chunk, chunk, 0)
    root_rows = lax.ppermute(root_rows, ("row", "col"), pairs)

    updates = mul(couple_sep, solved.astype(bf16)).astype(bf16).reshape(2 * COLS, chunk, sources)
    updates = lax.all_to_all(updates, ("row", "col"), 0, 0).astype(f32).sum(0)
    gram = jnp.pad(gram, ((0, 0), (0, sources - share)))
    both = gather(jnp.concatenate([updates, gram], 0), "sub", SUBS)
    rhs = root_rows - both[:, :chunk].sum(0)
    gram = both[:, chunk:, :share].reshape(2 * SUBS, chunk, share)
    applied = lax.dot_general(
        gram,
        jnp.broadcast_to(rhs[None], (2 * SUBS,) + rhs.shape),
        (((1,), (1,)), ((0,), (0,))),
        precision=fine,
        preferred_element_type=f32,
    )
    root_rows = sum_scatter(applied.reshape(SEPARATOR, sources), ("row", "col"), 2 * COLS)
    root_full = gather(root_rows.astype(bf16), ("row", "col"), 2 * COLS)
    value = solved - mul_t(couple_sep, root_full.reshape(SEPARATOR, sources))

    value = sum_scatter(mul_t(inverse, value, precision=fine), "col", COLS)
    root_rows = lax.ppermute(root_rows, ("row", "col"), [(j, i) for i, j in pairs])
    theirs = lax.ppermute(root_rows, "row", swap)
    root_part = jnp.where(
        row_id == 0,
        jnp.concatenate([root_rows, theirs], 0),
        jnp.concatenate([theirs, root_rows], 0),
    )
    value = after(value, root_part)
    later_low = gather(value.astype(bf16), "col", COLS).reshape(PANEL, sources)
    terms = lax.ppermute(mul(lower, later_low), "row", [(1, 0)])
    value = value - sum_scatter(mul_t(inverse, terms, precision=fine), "col", COLS)
    return value[None], root_part


def solution(mesh):
    return jax.shard_map(
        shards,
        mesh=mesh,
        in_specs=(
            P("sub", None, "col", "row"),
            P("sub", None, None),
            P("sub", ("row", "col"), None),
            P("sub", "row", "col", None),
            P("sub", None),
            P("col", None),
            P("sub", "row", None),
            P("col", None),
        ),
        out_specs=(P("sub", ("row", "col"), None), P("col", None)),
        check_vma=False,
    )
```

```python
import jax
import jax.numpy as jnp
from jax import lax
from jax.sharding import PartitionSpec as P

BLOCK = 256
PANEL = 2048
SEPARATOR = 1536
COLS = 16
SUBS = 8

f32 = jnp.float32
bf16 = jnp.bfloat16
fine = lax.Precision.HIGH
first_axes = (((0,), (0,)), ((), ()))


def mul(left, right, **kw):
    return jnp.dot(left, right, preferred_element_type=f32, **kw)


def mul_t(left, right, **kw):
    return lax.dot_general(left, right, first_axes, preferred_element_type=f32, **kw)


def after(value, other):
    return lax.optimization_barrier((value, other))[0]


def sum_scatter(partial, axes, count):
    parts = partial.reshape(count, -1, partial.shape[-1])
    here = lax.axis_index(axes)
    own = lax.dynamic_index_in_dim(parts, here, 0)
    others = lax.all_to_all(parts.astype(bf16), axes, 0, 0).astype(f32)
    index = lax.broadcasted_iota(jnp.int32, (count, 1, 1), 0)
    return jnp.where(index == here, own, others).sum(0)


def gather(chunk, axes, count):
    spread = jnp.broadcast_to(chunk[None], (count,) + chunk.shape)
    return lax.all_to_all(spread, axes, 0, 0)


def shards(
    factor_cols,
    block_pattern,
    diag_inverse,
    coupling_cols,
    separator_rows,
    root_inverse,
    right_side,
    root_right,
):
    table = block_pattern[0]
    inverse = diag_inverse[0]
    couple = coupling_cols[0, 0]
    rows_sep = separator_rows[0]
    row_id = lax.axis_index("row")
    col_id = lax.axis_index("col")
    sources = right_side.shape[-1]
    band_id = lax.axis_index(("sub", "row"))

    blocks = lax.dynamic_slice(table, (PANEL // BLOCK, col_id // 2), (PANEL // BLOCK, 1))
    lower = factor_cols[0, 0] * jnp.repeat(blocks[:, 0], BLOCK)[None, :].astype(bf16)
    width = lower.shape[0]

    own = mul(inverse, right_side[0], precision=fine)
    first_low = lax.ppermute(own.astype(bf16), "row", [(0, 1)])
    partial = mul_t(lower, first_low).astype(bf16)
    total = lax.all_to_all(partial.reshape(COLS, width, sources), "col", 0, 0)
    total = total.astype(f32).sum(0).astype(bf16)

    share = root_inverse.shape[0]
    band = SEPARATOR // (2 * SUBS)
    root_inverse = after(root_inverse, partial)
    gram = mul_t(
        root_inverse,
        lax.dynamic_slice_in_dim(root_inverse, band_id * band, band, 1),
        precision=fine,
    ).reshape(COLS, share, band)
    own_gram = lax.dynamic_index_in_dim(gram, col_id, 0)
    gram = jnp.pad(gram.astype(bf16), ((0, 0), (0, 0), (0, sources - band)))

    both = jnp.concatenate([jnp.broadcast_to(total[None], (COLS,) + total.shape), gram], 1)
    both = lax.all_to_all(both, "col", 0, 0)
    total = both[:, :width].reshape(PANEL, sources)
    solved = own - mul(inverse, total.astype(f32), precision=fine)
    chips = lax.broadcasted_iota(jnp.int32, (COLS, 1, 1), 0)
    gram = jnp.where(chips == col_id, own_gram, both[:, width:, :band].astype(f32)).sum(0)

    onehot = (jnp.arange(SEPARATOR)[:, None] == rows_sep[None, :]).astype(bf16)
    couple_sep = lax.dot_general(
        onehot, couple, (((1,), (1,)), ((), ())), preferred_element_type=f32
    ).astype(bf16)

    updates = mul(couple_sep, solved.astype(bf16)).astype(bf16).reshape(2 * SUBS, band, sources)
    updates = lax.all_to_all(updates, ("sub", "row"), 0, 0).astype(f32).sum(0)
    here = (band_id == col_id).astype(f32)
    low = (here * root_right - updates).astype(bf16)
    rhs = jnp.where(chips == col_id, here * root_right - updates, gather(low, "col", COLS)).sum(0)
    applied = mul(gram, rhs, precision=fine)
    half = share // 2
    kept = lax.dynamic_slice_in_dim(applied, row_id * half, half, 0)
    sent = lax.dynamic_slice_in_dim(applied, (1 - row_id) * half, half, 0)
    swap = [(0, 1), (1, 0)]
    kept = gather(kept + lax.ppermute(sent, "row", swap), "sub", SUBS).sum(0)
    other = lax.ppermute(kept, "row", swap)
    root_part = jnp.where(
        row_id == 0, jnp.concatenate([kept, other], 0), jnp.concatenate([other, kept], 0)
    )
    root_full = gather(root_part.astype(bf16), "col", COLS).reshape(SEPARATOR, sources)
    value = solved - mul_t(couple_sep, root_full)

    value = sum_scatter(mul_t(inverse, value, precision=fine), "col", COLS)
    later_low = gather(value.astype(bf16), "col", COLS).reshape(PANEL, sources)
    terms = lax.all_gather(mul(lower, later_low), "row")[1] * (row_id == 0).astype(f32)
    value = value - sum_scatter(mul_t(inverse, terms, precision=fine), "col", COLS)
    return value[None], root_part


def solution(mesh):
    return jax.shard_map(
        shards,
        mesh=mesh,
        in_specs=(
            P("sub", None, "col", "row"),
            P("sub", None, None),
            P("sub", ("row", "col"), None),
            P("sub", "row", "col", None),
            P("sub", None),
            P("col", None),
            P("sub", "row", None),
            P("col", None),
        ),
        out_specs=(P("sub", ("row", "col"), None), P("col", None)),
        check_vma=False,
    )
```

```python
import jax
import jax.numpy as jnp
from jax import lax
from jax.sharding import PartitionSpec as P

BLOCK = 256
PANEL = 2048
SEPARATOR = 1536
COLS = 16
SUBS = 8

f32 = jnp.float32
bf16 = jnp.bfloat16
fine = lax.Precision.HIGH
first_axes = (((0,), (0,)), ((), ()))


def mul(left, right, **kw):
    return jnp.dot(left, right, preferred_element_type=f32, **kw)


def mul_t(left, right, **kw):
    return lax.dot_general(left, right, first_axes, preferred_element_type=f32, **kw)


def after(value, other):
    return lax.optimization_barrier((value, other))[0]


def sum_scatter(partial, axes, count):
    parts = partial.reshape(count, -1, partial.shape[-1])
    here = lax.axis_index(axes)
    own = lax.dynamic_index_in_dim(parts, here, 0)
    others = lax.all_to_all(parts.astype(bf16), axes, 0, 0).astype(f32)
    index = lax.broadcasted_iota(jnp.int32, (count, 1, 1), 0)
    return jnp.where(index == here, own, others).sum(0)


def gather(chunk, axes, count):
    spread = jnp.broadcast_to(chunk[None], (count,) + chunk.shape)
    return lax.all_to_all(spread, axes, 0, 0)


def shards(
    factor_cols,
    block_pattern,
    diag_inverse,
    coupling_cols,
    separator_rows,
    root_inverse,
    right_side,
    root_right,
):
    table = block_pattern[0]
    inverse = diag_inverse[0]
    couple = coupling_cols[0, 0]
    rows_sep = separator_rows[0]
    row_id = lax.axis_index("row")
    col_id = lax.axis_index("col")
    sources = right_side.shape[-1]
    band_id = lax.axis_index(("row", "sub"))
    sub_id = lax.axis_index("sub")

    blocks = lax.dynamic_slice(table, (PANEL // BLOCK, col_id // 2), (PANEL // BLOCK, 1))
    lower = factor_cols[0, 0] * jnp.repeat(blocks[:, 0], BLOCK)[None, :].astype(bf16)
    width = lower.shape[0]

    own = mul(inverse, right_side[0], precision=fine)
    first_low = lax.ppermute(own.astype(bf16), "row", [(0, 1)])
    partial = mul_t(lower, first_low).astype(bf16)
    total = lax.all_to_all(partial.reshape(COLS, width, sources), "col", 0, 0)
    total = total.astype(f32).sum(0).astype(bf16)

    share = root_inverse.shape[0]
    band = SEPARATOR // (2 * SUBS)
    root_inverse = after(root_inverse, partial)
    gram = mul_t(
        root_inverse,
        lax.dynamic_slice_in_dim(root_inverse, band_id * band, band, 1),
        precision=fine,
    ).reshape(COLS, share, band)
    own_gram = lax.dynamic_index_in_dim(gram, col_id, 0)
    gram = jnp.pad(gram.astype(bf16), ((0, 0), (0, 0), (0, sources - band)))

    chunk = share // 2
    pairs = [
        (core * COLS + chip, (chip // 8) * COLS + 2 * (chip % 8) + core)
        for core in range(2)
        for chip in range(COLS)
    ]
    root_rows = lax.dynamic_slice_in_dim(after(root_right, partial), row_id * chunk, chunk, 0)
    root_rows = lax.ppermute(root_rows, ("row", "col"), pairs)
    both = jnp.concatenate([jnp.broadcast_to(total[None], (COLS,) + total.shape), gram], 1)
    both = lax.all_to_all(both, "col", 0, 0)
    total = both[:, :width].reshape(PANEL, sources)
    solved = after(own, root_rows) - mul(inverse, total.astype(f32), precision=fine)
    chips = lax.broadcasted_iota(jnp.int32, (COLS, 1, 1), 0)
    gram = jnp.where(chips == col_id, own_gram, both[:, width:, :band].astype(f32)).sum(0)

    onehot = (jnp.arange(SEPARATOR)[:, None] == rows_sep[None, :]).astype(bf16)
    couple_sep = lax.dot_general(
        onehot, couple, (((1,), (1,)), ((), ())), preferred_element_type=f32
    ).astype(bf16)

    gram = gram.T
    for step in (1, 2, 4):
        if step == 2:
            gram_pair = gram
        if step == 4:
            root_rows = after(root_rows, gram)
        other = lax.ppermute(gram, "sub", [(i, i ^ step) for i in range(SUBS)])
        gram = jnp.where(
            sub_id & step == 0,
            jnp.concatenate([gram, other], 0),
            jnp.concatenate([other, gram], 0),
        )

    updates = mul(couple_sep, solved.astype(bf16)).astype(bf16).reshape(2 * COLS, chunk, sources)
    updates = after(lax.all_to_all(updates, ("row", "col"), 0, 0), gram_pair)
    updates = updates.astype(f32).sum(0)
    updates = gather(updates, "sub", SUBS).sum(0)
    rhs = gather(root_rows - updates, "col", COLS).reshape(SEPARATOR // 2, sources)
    root_part = lax.all_gather(mul_t(gram, rhs, precision=fine), "row").sum(0)
    root_full = gather(root_part.astype(bf16), "col", COLS).reshape(SEPARATOR, sources)
    value = solved - mul_t(couple_sep, root_full)

    value = sum_scatter(mul_t(inverse, value, precision=fine), "col", COLS)
    later_low = gather(value.astype(bf16), "col", COLS).reshape(PANEL, sources)
    terms = lax.all_gather(mul(lower, later_low), "row")[1] * (row_id == 0).astype(f32)
    value = value - sum_scatter(mul_t(inverse, terms, precision=fine), "col", COLS)
    return value[None], root_part


def solution(mesh):
    return jax.shard_map(
        shards,
        mesh=mesh,
        in_specs=(
            P("sub", None, "col", "row"),
            P("sub", None, None),
            P("sub", ("row", "col"), None),
            P("sub", "row", "col", None),
            P("sub", None),
            P("col", None),
            P("sub", "row", None),
            P("col", None),
        ),
        out_specs=(P("sub", ("row", "col"), None), P("col", None)),
        check_vma=False,
    )
```

```python
import jax
import jax.numpy as jnp
from jax import lax
from jax.sharding import PartitionSpec as P

BLOCK = 256
PANEL = 2048
SEPARATOR = 1536
COLS = 16
SUBS = 8

f32 = jnp.float32
bf16 = jnp.bfloat16
fine = lax.Precision.HIGH
first_axes = (((0,), (0,)), ((), ()))


def mul(left, right, **kw):
    return jnp.dot(left, right, preferred_element_type=f32, **kw)


def mul_t(left, right, **kw):
    return lax.dot_general(left, right, first_axes, preferred_element_type=f32, **kw)


def after(value, other):
    return lax.optimization_barrier((value, other))[0]


def sum_scatter(partial, axes, count):
    parts = partial.reshape(count, -1, partial.shape[-1])
    here = lax.axis_index(axes)
    own = lax.dynamic_index_in_dim(parts, here, 0)
    others = lax.all_to_all(parts.astype(bf16), axes, 0, 0).astype(f32)
    index = lax.broadcasted_iota(jnp.int32, (count, 1, 1), 0)
    return jnp.where(index == here, own, others).sum(0)


def gather(chunk, axes, count):
    spread = jnp.broadcast_to(chunk[None], (count,) + chunk.shape)
    return lax.all_to_all(spread, axes, 0, 0)


def shards(
    factor_cols,
    block_pattern,
    diag_inverse,
    coupling_cols,
    separator_rows,
    root_inverse,
    right_side,
    root_right,
):
    table = block_pattern[0]
    inverse = diag_inverse[0]
    couple = coupling_cols[0, 0]
    rows_sep = separator_rows[0]
    row_id = lax.axis_index("row")
    col_id = lax.axis_index("col")
    sources = right_side.shape[-1]
    sub_id = lax.axis_index("sub")
    band_id = row_id * SUBS + sub_id % 2 * 4 + sub_id // 2 % 2 * 2 + sub_id // 4

    blocks = lax.dynamic_slice(table, (PANEL // BLOCK, col_id // 2), (PANEL // BLOCK, 1))
    lower = factor_cols[0, 0] * jnp.repeat(blocks[:, 0], BLOCK)[None, :].astype(bf16)
    width = lower.shape[0]

    own = mul(inverse, right_side[0], precision=fine)
    first_low = lax.ppermute(own.astype(bf16), "row", [(0, 1)])
    partial = mul_t(lower, first_low).astype(bf16)
    total = lax.all_to_all(partial.reshape(COLS, width, sources), "col", 0, 0)
    total = total.astype(f32).sum(0).astype(bf16)

    share = root_inverse.shape[0]
    band = SEPARATOR // (2 * SUBS)
    root_inverse = after(root_inverse, partial)
    gram = mul_t(
        root_inverse,
        lax.dynamic_slice_in_dim(root_inverse, band_id * band, band, 1),
        precision=fine,
    ).reshape(COLS, share, band)
    own_gram = lax.dynamic_index_in_dim(gram, col_id, 0)
    gram = jnp.pad(gram.astype(bf16), ((0, 0), (0, 0), (0, sources - band)))

    chunk = share // 2
    pairs = [
        (core * COLS + chip, (chip // 8) * COLS + 2 * (chip % 8) + core)
        for core in range(2)
        for chip in range(COLS)
    ]
    root_rows = lax.dynamic_slice_in_dim(after(root_right, partial), row_id * chunk, chunk, 0)
    root_rows = root_rows_sent = lax.ppermute(root_rows, ("row", "col"), pairs)
    both = jnp.concatenate([jnp.broadcast_to(total[None], (COLS,) + total.shape), gram], 1)
    both = lax.all_to_all(both, "col", 0, 0)
    total = both[:, :width].reshape(PANEL, sources)
    solved = own - mul(inverse, total.astype(f32), precision=fine)
    chips = lax.broadcasted_iota(jnp.int32, (COLS, 1, 1), 0)
    gram = jnp.where(chips == col_id, own_gram, both[:, width:, :band].astype(f32)).sum(0)

    onehot = (jnp.arange(SEPARATOR)[:, None] == rows_sep[None, :]).astype(bf16)
    couple_sep = lax.dot_general(
        onehot, couple, (((1,), (1,)), ((), ())), preferred_element_type=f32
    ).astype(bf16)

    gram = gram.T
    for step in (4, 2, 1):
        if step == 2:
            gram_pair = gram
        if step == 1:
            root_rows = after(root_rows, gram)
        other = lax.ppermute(gram, "sub", [(i, i ^ step) for i in range(SUBS)])
        gram = jnp.where(
            sub_id & step == 0,
            jnp.concatenate([gram, other], 0),
            jnp.concatenate([other, gram], 0),
        )

    updates = mul(couple_sep, solved.astype(bf16)).astype(bf16).reshape(2 * COLS, chunk, sources)
    updates = after(lax.all_to_all(updates, ("row", "col"), 0, 0), (gram_pair, root_rows_sent))
    updates = updates.astype(f32).sum(0)
    updates = gather(updates, "sub", SUBS).sum(0)
    rhs = gather(root_rows - updates, "col", COLS).reshape(SEPARATOR // 2, sources)
    root_part = lax.all_gather(mul_t(gram, rhs, precision=fine), "row").sum(0)
    root_full = gather(root_part.astype(bf16), "col", COLS).reshape(SEPARATOR, sources)
    value = solved - mul_t(couple_sep, root_full)

    value = sum_scatter(mul_t(inverse, value, precision=fine), "col", COLS)
    later_low = gather(value.astype(bf16), "col", COLS).reshape(PANEL, sources)
    terms = lax.all_gather(mul(lower, later_low), "row")[1] * (row_id == 0).astype(f32)
    value = value - sum_scatter(mul_t(inverse, terms, precision=fine), "col", COLS)
    return value[None], root_part


def solution(mesh):
    return jax.shard_map(
        shards,
        mesh=mesh,
        in_specs=(
            P("sub", None, "col", "row"),
            P("sub", None, None),
            P("sub", ("row", "col"), None),
            P("sub", "row", "col", None),
            P("sub", None),
            P("col", None),
            P("sub", "row", None),
            P("col", None),
        ),
        out_specs=(P("sub", ("row", "col"), None), P("col", None)),
        check_vma=False,
    )
```

```python
import jax
import jax.numpy as jnp
from jax import lax
from jax.sharding import PartitionSpec as P

BLOCK = 256
PANEL = 2048
SEPARATOR = 1536
COLS = 16
SUBS = 8

f32 = jnp.float32
bf16 = jnp.bfloat16
fine = lax.Precision.HIGH
first_axes = (((0,), (0,)), ((), ()))


def mul(left, right, **kw):
    return jnp.dot(left, right, preferred_element_type=f32, **kw)


def mul_t(left, right, **kw):
    return lax.dot_general(left, right, first_axes, preferred_element_type=f32, **kw)


def after(value, other):
    return lax.optimization_barrier((value, other))[0]


def collect(blocks, step, sub_id):
    other = lax.ppermute(blocks, "sub", [(i, i ^ step) for i in range(SUBS)])
    return jnp.where(
        sub_id & step == 0,
        jnp.concatenate([blocks, other], 0),
        jnp.concatenate([other, blocks], 0),
    )


def sum_scatter(partial, axes, count):
    parts = partial.reshape(count, -1, partial.shape[-1])
    here = lax.axis_index(axes)
    own = lax.dynamic_index_in_dim(parts, here, 0)
    others = lax.all_to_all(parts.astype(bf16), axes, 0, 0).astype(f32)
    index = lax.broadcasted_iota(jnp.int32, (count, 1, 1), 0)
    return jnp.where(index == here, own, others).sum(0)


def gather(chunk, axes, count):
    spread = jnp.broadcast_to(chunk[None], (count,) + chunk.shape)
    return lax.all_to_all(spread, axes, 0, 0)


def shards(
    factor_cols,
    block_pattern,
    diag_inverse,
    coupling_cols,
    separator_rows,
    root_inverse,
    right_side,
    root_right,
):
    table = block_pattern[0]
    inverse = diag_inverse[0]
    couple = coupling_cols[0, 0]
    rows_sep = separator_rows[0]
    row_id = lax.axis_index("row")
    col_id = lax.axis_index("col")
    sources = right_side.shape[-1]
    sub_id = lax.axis_index("sub")
    band_id = row_id * SUBS + sub_id % 2 * 4 + sub_id // 2 % 2 * 2 + sub_id // 4

    blocks = lax.dynamic_slice(table, (PANEL // BLOCK, col_id // 2), (PANEL // BLOCK, 1))
    lower = factor_cols[0, 0] * jnp.repeat(blocks[:, 0], BLOCK)[None, :].astype(bf16)
    width = lower.shape[0]

    own = mul(inverse, right_side[0], precision=fine)
    first_low = lax.ppermute(own.astype(bf16), "row", [(0, 1)])
    partial = mul_t(lower, first_low).astype(bf16)
    total = lax.all_to_all(partial.reshape(COLS, width, sources), "col", 0, 0)
    total = total.astype(f32).sum(0).astype(bf16)

    share = root_inverse.shape[0]
    band = SEPARATOR // (2 * SUBS)
    root_inverse = after(root_inverse, partial)
    gram = mul_t(
        root_inverse,
        lax.dynamic_slice_in_dim(root_inverse, band_id * band, band, 1),
        precision=fine,
    ).reshape(COLS, share, band)
    own_gram = lax.dynamic_index_in_dim(gram, col_id, 0)
    gram = jnp.pad(gram.astype(bf16), ((0, 0), (0, 0), (0, sources - band)))

    chunk = share // 2
    pairs = [
        (core * COLS + chip, (chip // 8) * COLS + 2 * (chip % 8) + core)
        for core in range(2)
        for chip in range(COLS)
    ]
    root_rows = lax.dynamic_slice_in_dim(after(root_right, partial), row_id * chunk, chunk, 0)
    root_rows = lax.ppermute(root_rows, ("row", "col"), pairs)
    both = jnp.concatenate([jnp.broadcast_to(total[None], (COLS,) + total.shape), gram], 1)
    both = lax.all_to_all(both, "col", 0, 0)
    total = both[:, :width].reshape(PANEL, sources)
    solved = own - mul(inverse, total.astype(f32), precision=fine)
    chips = lax.broadcasted_iota(jnp.int32, (COLS, 1, 1), 0)
    gram = jnp.where(chips == col_id, own_gram, both[:, width:, :band].astype(f32)).sum(0)

    onehot = (jnp.arange(SEPARATOR)[:, None] == rows_sep[None, :]).astype(bf16)
    couple_sep = lax.dot_general(
        onehot, couple, (((1,), (1,)), ((), ())), preferred_element_type=f32
    ).astype(bf16)

    gram = collect(gram.T, 4, sub_id)
    updates = mul(couple_sep, solved.astype(bf16)).astype(bf16).reshape(2 * COLS, chunk, sources)
    updates = after(lax.all_to_all(updates, ("row", "col"), 0, 0), (gram, root_rows))
    updates = updates.astype(f32).sum(0)
    updates = gather(updates, "sub", SUBS).sum(0)
    gram = collect(collect(after(gram, updates), 2, sub_id), 1, sub_id)
    rhs = gather(root_rows - updates, "col", COLS).reshape(SEPARATOR // 2, sources)
    root_part = lax.all_gather(mul_t(gram, rhs, precision=fine), "row").sum(0)
    root_full = gather(root_part.astype(bf16), "col", COLS).reshape(SEPARATOR, sources)
    value = solved - mul_t(couple_sep, root_full)

    value = sum_scatter(mul_t(inverse, value, precision=fine), "col", COLS)
    later_low = gather(value.astype(bf16), "col", COLS).reshape(PANEL, sources)
    terms = lax.all_gather(mul(lower, later_low), "row")[1] * (row_id == 0).astype(f32)
    value = value - sum_scatter(mul_t(inverse, terms, precision=fine), "col", COLS)
    return value[None], root_part


def solution(mesh):
    return jax.shard_map(
        shards,
        mesh=mesh,
        in_specs=(
            P("sub", None, "col", "row"),
            P("sub", None, None),
            P("sub", ("row", "col"), None),
            P("sub", "row", "col", None),
            P("sub", None),
            P("col", None),
            P("sub", "row", None),
            P("col", None),
        ),
        out_specs=(P("sub", ("row", "col"), None), P("col", None)),
        check_vma=False,
    )
```

```python
import jax
import jax.numpy as jnp
from jax import lax
from jax.sharding import PartitionSpec as P

BLOCK = 256
PANEL = 2048
SEPARATOR = 1536
COLS = 16
SUBS = 8

f32 = jnp.float32
bf16 = jnp.bfloat16
fine = lax.Precision.HIGH
first_axes = (((0,), (0,)), ((), ()))


def mul(left, right, **kw):
    return jnp.dot(left, right, preferred_element_type=f32, **kw)


def mul_t(left, right, **kw):
    return lax.dot_general(left, right, first_axes, preferred_element_type=f32, **kw)


def after(value, other):
    return lax.optimization_barrier((value, other))[0]


def collect(blocks, step, sub_id):
    other = lax.ppermute(blocks, "sub", [(i, i ^ step) for i in range(SUBS)])
    return jnp.where(
        sub_id & step == 0,
        jnp.concatenate([blocks, other], 0),
        jnp.concatenate([other, blocks], 0),
    )


def sum_scatter(partial, axes, count):
    parts = partial.reshape(count, -1, partial.shape[-1])
    here = lax.axis_index(axes)
    own = lax.dynamic_index_in_dim(parts, here, 0)
    others = lax.all_to_all(parts.astype(bf16), axes, 0, 0).astype(f32)
    index = lax.broadcasted_iota(jnp.int32, (count, 1, 1), 0)
    return jnp.where(index == here, own, others).sum(0)


def gather(chunk, axes, count):
    spread = jnp.broadcast_to(chunk[None], (count,) + chunk.shape)
    return lax.all_to_all(spread, axes, 0, 0)


def shards(
    factor_cols,
    block_pattern,
    diag_inverse,
    coupling_cols,
    separator_rows,
    root_inverse,
    right_side,
    root_right,
):
    table = block_pattern[0]
    inverse = diag_inverse[0]
    couple = coupling_cols[0, 0]
    rows_sep = separator_rows[0]
    row_id = lax.axis_index("row")
    col_id = lax.axis_index("col")
    sources = right_side.shape[-1]
    sub_id = lax.axis_index("sub")
    band_id = row_id * SUBS + sub_id % 2 * 4 + sub_id // 2 % 2 * 2 + sub_id // 4

    blocks = lax.dynamic_slice(table, (PANEL // BLOCK, col_id // 2), (PANEL // BLOCK, 1))
    lower = factor_cols[0, 0] * jnp.repeat(blocks[:, 0], BLOCK)[None, :].astype(bf16)
    width = lower.shape[0]

    own = mul(inverse, right_side[0], precision=fine)
    first_low = lax.ppermute(own.astype(bf16), "row", [(0, 1)])
    partial = mul_t(lower, first_low).astype(bf16)

    share = root_inverse.shape[0]
    band = SEPARATOR // (2 * SUBS)
    gram = mul_t(
        root_inverse,
        lax.dynamic_slice_in_dim(root_inverse, band_id * band, band, 1),
        precision=fine,
    ).reshape(COLS, share, band)
    own_gram = lax.dynamic_index_in_dim(gram, col_id, 0)
    gram = jnp.pad(gram.astype(bf16), ((0, 0), (0, 0), (0, sources - band)))

    both = jnp.concatenate([partial.reshape(COLS, width, sources), gram], 1)
    both = lax.all_to_all(both, "col", 0, 0)
    total = both[:, :width].astype(f32).sum(0).astype(bf16)
    chips = lax.broadcasted_iota(jnp.int32, (COLS, 1, 1), 0)
    gram = jnp.where(chips == col_id, own_gram, both[:, width:, :band].astype(f32)).sum(0)
    gram = collect(gram.T, 4, sub_id)

    chunk = share // 2
    pairs = [
        (core * COLS + chip, (chip // 8) * COLS + 2 * (chip % 8) + core)
        for core in range(2)
        for chip in range(COLS)
    ]
    root_rows = lax.dynamic_slice_in_dim(after(root_right, partial), row_id * chunk, chunk, 0)
    root_rows = lax.ppermute(root_rows, ("row", "col"), pairs)

    total = after(gather(total, "col", COLS), gram).reshape(PANEL, sources)
    solved = own - mul(inverse, total.astype(f32), precision=fine)

    onehot = (jnp.arange(SEPARATOR)[:, None] == rows_sep[None, :]).astype(bf16)
    couple_sep = lax.dot_general(
        onehot, couple, (((1,), (1,)), ((), ())), preferred_element_type=f32
    ).astype(bf16)

    gram = collect(gram, 2, sub_id)
    updates = mul(couple_sep, solved.astype(bf16)).astype(bf16).reshape(2 * COLS, chunk, sources)
    updates = after(lax.all_to_all(updates, ("row", "col"), 0, 0), (gram, root_rows))
    updates = updates.astype(f32).sum(0)
    updates = gather(updates, "sub", SUBS).sum(0)
    gram = collect(after(gram, updates), 1, sub_id)
    rhs = gather(root_rows - updates, "col", COLS).reshape(SEPARATOR // 2, sources)
    root_part = lax.all_gather(mul_t(gram, rhs, precision=fine), "row").sum(0)
    root_full = gather(root_part.astype(bf16), "col", COLS).reshape(SEPARATOR, sources)
    value = solved - mul_t(couple_sep, root_full)

    value = sum_scatter(mul_t(inverse, value, precision=fine), "col", COLS)
    later_low = gather(value.astype(bf16), "col", COLS).reshape(PANEL, sources)
    terms = lax.all_gather(mul(lower, later_low), "row")[1] * (row_id == 0).astype(f32)
    value = value - sum_scatter(mul_t(inverse, terms, precision=fine), "col", COLS)
    return value[None], root_part


def solution(mesh):
    return jax.shard_map(
        shards,
        mesh=mesh,
        in_specs=(
            P("sub", None, "col", "row"),
            P("sub", None, None),
            P("sub", ("row", "col"), None),
            P("sub", "row", "col", None),
            P("sub", None),
            P("col", None),
            P("sub", "row", None),
            P("col", None),
        ),
        out_specs=(P("sub", ("row", "col"), None), P("col", None)),
        check_vma=False,
    )
```

```python
import jax
import jax.numpy as jnp
from jax import lax
from jax.sharding import PartitionSpec as P

BLOCK = 256
PANEL = 2048
SEPARATOR = 1536
COLS = 16
SUBS = 8

f32 = jnp.float32
bf16 = jnp.bfloat16
fine = lax.Precision.HIGH
first_axes = (((0,), (0,)), ((), ()))


def mul(left, right, **kw):
    return jnp.dot(left, right, preferred_element_type=f32, **kw)


def mul_t(left, right, **kw):
    return lax.dot_general(left, right, first_axes, preferred_element_type=f32, **kw)


def after(value, other):
    return lax.optimization_barrier((value, other))[0]


def collect(blocks, step, sub_id):
    other = lax.ppermute(blocks, "sub", [(i, i ^ step) for i in range(SUBS)])
    return jnp.where(
        sub_id & step == 0,
        jnp.concatenate([blocks, other], 0),
        jnp.concatenate([other, blocks], 0),
    )


def sum_scatter(partial, axes, count):
    parts = partial.reshape(count, -1, partial.shape[-1])
    here = lax.axis_index(axes)
    own = lax.dynamic_index_in_dim(parts, here, 0)
    low, own = lax.optimization_barrier((parts.astype(bf16), own))
    others = lax.all_to_all(low, axes, 0, 0).astype(f32)
    index = lax.broadcasted_iota(jnp.int32, (count, 1, 1), 0)
    return jnp.where(index == here, own, others).sum(0)


def gather(chunk, axes, count):
    spread = jnp.broadcast_to(chunk[None], (count,) + chunk.shape)
    return lax.all_to_all(spread, axes, 0, 0)


def shards(
    factor_cols,
    block_pattern,
    diag_inverse,
    coupling_cols,
    separator_rows,
    root_inverse,
    right_side,
    root_right,
):
    table = block_pattern[0]
    inverse = diag_inverse[0]
    couple = coupling_cols[0, 0]
    rows_sep = separator_rows[0]
    row_id = lax.axis_index("row")
    col_id = lax.axis_index("col")
    sources = right_side.shape[-1]
    sub_id = lax.axis_index("sub")
    band_id = row_id * SUBS + sub_id % 2 * 4 + sub_id // 2 % 2 * 2 + sub_id // 4

    blocks = lax.dynamic_slice(table, (PANEL // BLOCK, col_id // 2), (PANEL // BLOCK, 1))
    lower = factor_cols[0, 0] * jnp.repeat(blocks[:, 0], BLOCK)[None, :].astype(bf16)
    width = lower.shape[0]

    own = mul(inverse, right_side[0], precision=fine)
    first_low = lax.ppermute(own.astype(bf16), "row", [(0, 1)])
    partial = mul_t(lower, first_low).astype(bf16)

    share = root_inverse.shape[0]
    band = SEPARATOR // (2 * SUBS)
    gram = mul_t(
        root_inverse,
        lax.dynamic_slice_in_dim(root_inverse, band_id * band, band, 1),
        precision=fine,
    ).reshape(COLS, share, band)
    own_gram = lax.dynamic_index_in_dim(gram, col_id, 0)
    gram = jnp.pad(gram.astype(bf16), ((0, 0), (0, 0), (0, sources - band)))

    both = jnp.concatenate([partial.reshape(COLS, width, sources), gram], 1)
    both = lax.all_to_all(both, "col", 0, 0)
    total = both[:, :width].astype(f32).sum(0).astype(bf16)
    chips = lax.broadcasted_iota(jnp.int32, (COLS, 1, 1), 0)
    gram = jnp.where(chips == col_id, own_gram, both[:, width:, :band].astype(f32)).sum(0)
    gram = collect(gram.T, 4, sub_id)

    chunk = share // 2
    pairs = [
        (core * COLS + chip, (chip // 8) * COLS + 2 * (chip % 8) + core)
        for core in range(2)
        for chip in range(COLS)
    ]
    root_rows = lax.dynamic_slice_in_dim(after(root_right, partial), row_id * chunk, chunk, 0)
    root_rows = lax.ppermute(root_rows, ("row", "col"), pairs)

    total = after(gather(total, "col", COLS), gram).reshape(PANEL, sources)
    solved = own - mul(inverse, total.astype(f32), precision=fine)

    onehot = (jnp.arange(SEPARATOR)[:, None] == rows_sep[None, :]).astype(bf16)
    couple_sep = lax.dot_general(
        onehot, couple, (((1,), (1,)), ((), ())), preferred_element_type=f32
    ).astype(bf16)

    gram = collect(gram, 2, sub_id)
    updates = mul(couple_sep, solved.astype(bf16)).astype(bf16).reshape(2 * COLS, chunk, sources)
    updates = after(lax.all_to_all(updates, ("row", "col"), 0, 0), (gram, root_rows))
    updates = updates.astype(f32).sum(0)
    updates = gather(updates, "sub", SUBS).sum(0)
    gram = collect(after(gram, updates), 1, sub_id)
    gram, first = lax.optimization_barrier((gram, (row_id == 0).astype(f32)))
    rhs = gather(root_rows - updates, "col", COLS).reshape(SEPARATOR // 2, sources)
    root_part = lax.all_gather(mul_t(gram, rhs, precision=fine), "row").sum(0)
    root_full = gather(root_part.astype(bf16), "col", COLS).reshape(SEPARATOR, sources)
    value = solved - mul_t(couple_sep, root_full)

    value = sum_scatter(mul_t(inverse, value, precision=fine), "col", COLS)
    later_low = gather(value.astype(bf16), "col", COLS).reshape(PANEL, sources)
    terms = lax.all_gather(mul(lower, later_low), "row")[1] * first
    value = value - sum_scatter(mul_t(inverse, terms, precision=fine), "col", COLS)
    return value[None], root_part


def solution(mesh):
    return jax.shard_map(
        shards,
        mesh=mesh,
        in_specs=(
            P("sub", None, "col", "row"),
            P("sub", None, None),
            P("sub", ("row", "col"), None),
            P("sub", "row", "col", None),
            P("sub", None),
            P("col", None),
            P("sub", "row", None),
            P("col", None),
        ),
        out_specs=(P("sub", ("row", "col"), None), P("col", None)),
        check_vma=False,
    )
```

```python
import jax
import jax.numpy as jnp
from jax import lax
from jax.sharding import PartitionSpec as P

BLOCK = 256
PANEL = 2048
SEPARATOR = 1536
COLS = 16
SUBS = 8

f32 = jnp.float32
bf16 = jnp.bfloat16
fine = lax.Precision.HIGH
first_axes = (((0,), (0,)), ((), ()))


def mul(left, right, **kw):
    return jnp.dot(left, right, preferred_element_type=f32, **kw)


def mul_t(left, right, **kw):
    return lax.dot_general(left, right, first_axes, preferred_element_type=f32, **kw)


def after(value, other):
    return lax.optimization_barrier((value, other))[0]


def collect(blocks, step, sub_id):
    other = lax.ppermute(blocks, "sub", [(i, i ^ step) for i in range(SUBS)])
    return jnp.where(
        sub_id & step == 0,
        jnp.concatenate([blocks, other], 0),
        jnp.concatenate([other, blocks], 0),
    )


def sum_scatter(partial, axes, count):
    parts = partial.reshape(count, -1, partial.shape[-1])
    here = lax.axis_index(axes)
    own = lax.dynamic_index_in_dim(parts, here, 0)
    low, own = lax.optimization_barrier((parts.astype(bf16), own))
    others = lax.all_to_all(low, axes, 0, 0).astype(f32)
    index = lax.broadcasted_iota(jnp.int32, (count, 1, 1), 0)
    return jnp.where(index == here, own, others).sum(0)


def gather(chunk, axes, count):
    spread = jnp.broadcast_to(chunk[None], (count,) + chunk.shape)
    return lax.all_to_all(spread, axes, 0, 0)


def shards(
    factor_cols,
    block_pattern,
    diag_inverse,
    coupling_cols,
    separator_rows,
    root_inverse,
    right_side,
    root_right,
):
    table = block_pattern[0]
    inverse = diag_inverse[0]
    couple = coupling_cols[0, 0]
    rows_sep = separator_rows[0]
    row_id = lax.axis_index("row")
    col_id = lax.axis_index("col")
    sources = right_side.shape[-1]
    sub_id = lax.axis_index("sub")
    band_id = row_id * SUBS + sub_id % 2 * 4 + sub_id // 2 % 2 * 2 + sub_id // 4

    blocks = lax.dynamic_slice(table, (PANEL // BLOCK, col_id // 2), (PANEL // BLOCK, 1))
    lower = factor_cols[0, 0] * jnp.repeat(blocks[:, 0], BLOCK)[None, :].astype(bf16)
    width = lower.shape[0]

    own = mul(inverse, right_side[0], precision=fine)
    first_low = lax.ppermute(own.astype(bf16), "row", [(0, 1)])
    partial = mul_t(lower, first_low).astype(bf16)

    share = root_inverse.shape[0]
    band = SEPARATOR // (2 * SUBS)
    gram = mul_t(
        root_inverse,
        lax.dynamic_slice_in_dim(root_inverse, band_id * band, band, 1),
        precision=fine,
    ).reshape(COLS, share, band)
    own_gram = gram
    gram = jnp.pad(gram.astype(bf16), ((0, 0), (0, 0), (0, sources - band)))

    both = jnp.concatenate([partial.reshape(COLS, width, sources), gram], 1)
    both = lax.all_to_all(both, "col", 0, 0)
    total = both[:, :width].astype(f32).sum(0).astype(bf16)
    here, own_gram = after((col_id, own_gram), total)
    own_gram = lax.dynamic_index_in_dim(own_gram, here, 0)
    chips = lax.broadcasted_iota(jnp.int32, (COLS, 1, 1), 0)
    gram = jnp.where(chips == here, own_gram, both[:, width:, :band].astype(f32)).sum(0)
    gram = collect(gram.T, 4, sub_id)

    chunk = share // 2
    pairs = [
        (core * COLS + chip, (chip // 8) * COLS + 2 * (chip % 8) + core)
        for core in range(2)
        for chip in range(COLS)
    ]
    root_rows = lax.dynamic_slice_in_dim(after(root_right, partial), row_id * chunk, chunk, 0)
    root_rows = lax.ppermute(root_rows, ("row", "col"), pairs)

    total = after(gather(total, "col", COLS), gram).reshape(PANEL, sources)
    solved = own - mul(inverse, total.astype(f32), precision=fine)

    onehot = (jnp.arange(SEPARATOR)[:, None] == rows_sep[None, :]).astype(bf16)
    couple_sep = lax.dot_general(
        onehot, couple, (((1,), (1,)), ((), ())), preferred_element_type=f32
    ).astype(bf16)

    gram = collect(gram, 2, sub_id)
    updates = mul(couple_sep, solved.astype(bf16)).astype(bf16).reshape(2 * COLS, chunk, sources)
    updates = after(lax.all_to_all(updates, ("row", "col"), 0, 0), (gram, root_rows))
    updates = updates.astype(f32).sum(0)
    updates = gather(updates, "sub", SUBS).sum(0)
    gram = collect(after(gram, updates), 1, sub_id)
    gram, first = lax.optimization_barrier((gram, (row_id == 0).astype(f32)))
    rhs = gather(root_rows - updates, "col", COLS).reshape(SEPARATOR // 2, sources)
    root_part = lax.all_gather(mul_t(gram, rhs, precision=fine), "row").sum(0)
    root_full = gather(root_part.astype(bf16), "col", COLS).reshape(SEPARATOR, sources)
    value = solved - mul_t(couple_sep, root_full)

    value = sum_scatter(mul_t(inverse, value, precision=fine), "col", COLS)
    later_low = gather(value.astype(bf16), "col", COLS).reshape(PANEL, sources)
    terms = lax.all_gather(mul(lower, later_low), "row")[1] * first
    value = value - sum_scatter(mul_t(inverse, terms, precision=fine), "col", COLS)
    return value[None], root_part


def solution(mesh):
    return jax.shard_map(
        shards,
        mesh=mesh,
        in_specs=(
            P("sub", None, "col", "row"),
            P("sub", None, None),
            P("sub", ("row", "col"), None),
            P("sub", "row", "col", None),
            P("sub", None),
            P("col", None),
            P("sub", "row", None),
            P("col", None),
        ),
        out_specs=(P("sub", ("row", "col"), None), P("col", None)),
        check_vma=False,
    )
```

```python
import jax
import jax.numpy as jnp
from jax import lax
from jax.sharding import PartitionSpec as P

BLOCK = 256
PANEL = 2048
SEPARATOR = 1536
COLS = 16
SUBS = 8

f32 = jnp.float32
bf16 = jnp.bfloat16
fine = lax.Precision.HIGH
first_axes = (((0,), (0,)), ((), ()))


def mul(left, right, **kw):
    return jnp.dot(left, right, preferred_element_type=f32, **kw)


def mul_t(left, right, **kw):
    return lax.dot_general(left, right, first_axes, preferred_element_type=f32, **kw)


def after(value, other):
    return lax.optimization_barrier((value, other))[0]


def collect(blocks, step, sub_id):
    other = lax.ppermute(blocks, "sub", [(i, i ^ step) for i in range(SUBS)])
    return jnp.where(
        sub_id & step == 0,
        jnp.concatenate([blocks, other], 0),
        jnp.concatenate([other, blocks], 0),
    )


def sum_scatter(partial, axes, count):
    parts = partial.reshape(count, -1, partial.shape[-1])
    here = lax.axis_index(axes)
    own = lax.dynamic_index_in_dim(parts, here, 0)
    low, own = lax.optimization_barrier((parts.astype(bf16), own))
    others = lax.all_to_all(low, axes, 0, 0).astype(f32)
    index = lax.broadcasted_iota(jnp.int32, (count, 1, 1), 0)
    return jnp.where(index == here, own, others).sum(0)


def gather(chunk, axes, count):
    spread = jnp.broadcast_to(chunk[None], (count,) + chunk.shape)
    return lax.all_to_all(spread, axes, 0, 0)


def shards(
    factor_cols,
    block_pattern,
    diag_inverse,
    coupling_cols,
    separator_rows,
    root_inverse,
    right_side,
    root_right,
):
    table = block_pattern[0]
    inverse = diag_inverse[0]
    couple = coupling_cols[0, 0]
    rows_sep = separator_rows[0]
    row_id = lax.axis_index("row")
    col_id = lax.axis_index("col")
    sources = right_side.shape[-1]
    sub_id = lax.axis_index("sub")
    band_id = row_id * SUBS + sub_id % 2 * 4 + sub_id // 2 % 2 * 2 + sub_id // 4

    blocks = lax.dynamic_slice(table, (PANEL // BLOCK, col_id // 2), (PANEL // BLOCK, 1))
    lower = factor_cols[0, 0] * jnp.repeat(blocks[:, 0], BLOCK)[None, :].astype(bf16)
    width = lower.shape[0]

    own = mul(inverse, right_side[0], precision=fine)
    first_low = lax.ppermute(own.astype(bf16), "row", [(0, 1)])
    partial = mul_t(lower, first_low).astype(bf16)

    share = root_inverse.shape[0]
    band = SEPARATOR // (2 * SUBS)
    gram = mul_t(
        root_inverse,
        lax.dynamic_slice_in_dim(root_inverse, band_id * band, band, 1),
        precision=fine,
    ).reshape(COLS, share, band)
    own_gram = lax.dynamic_index_in_dim(gram, col_id, 0)
    gram = jnp.pad(gram.astype(bf16), ((0, 0), (0, 0), (0, sources - band)))

    chunk = share // 2
    pairs = [
        (core * COLS + chip, (chip // 8) * COLS + 2 * (chip % 8) + core)
        for core in range(2)
        for chip in range(COLS)
    ]
    root_rows = lax.dynamic_slice_in_dim(after(root_right, partial), row_id * chunk, chunk, 0)
    root_rows = lax.ppermute(root_rows, ("row", "col"), pairs)

    both = jnp.concatenate([partial.reshape(COLS, width, sources), gram], 1)
    both = after(lax.all_to_all(both, "col", 0, 0), root_rows)
    total = both[:, :width].astype(f32).sum(0).astype(bf16)
    chips = lax.broadcasted_iota(jnp.int32, (COLS, 1, 1), 0)
    gram = jnp.where(chips == col_id, own_gram, both[:, width:, :band].astype(f32)).sum(0)
    gram = collect(gram.T, 4, sub_id)

    total = after(gather(total, "col", COLS), gram).reshape(PANEL, sources)
    solved = own - mul(inverse, total.astype(f32), precision=fine)

    onehot = (jnp.arange(SEPARATOR)[:, None] == rows_sep[None, :]).astype(bf16)
    couple_sep = lax.dot_general(
        onehot, couple, (((1,), (1,)), ((), ())), preferred_element_type=f32
    ).astype(bf16)

    gram = collect(gram, 2, sub_id)
    updates = mul(couple_sep, solved.astype(bf16)).astype(bf16).reshape(2 * COLS, chunk, sources)
    updates = after(lax.all_to_all(updates, ("row", "col"), 0, 0), gram)
    updates = updates.astype(f32).sum(0)
    updates = gather(updates, "sub", SUBS).sum(0)
    gram = collect(after(gram, updates), 1, sub_id)
    gram, first = lax.optimization_barrier((gram, (row_id == 0).astype(f32)))
    rhs = gather(root_rows - updates, "col", COLS).reshape(SEPARATOR // 2, sources)
    root_part = lax.all_gather(mul_t(gram, rhs, precision=fine), "row").sum(0)
    root_full = gather(root_part.astype(bf16), "col", COLS).reshape(SEPARATOR, sources)
    value = solved - mul_t(couple_sep, root_full)

    value = sum_scatter(mul_t(inverse, value, precision=fine), "col", COLS)
    later_low = gather(value.astype(bf16), "col", COLS).reshape(PANEL, sources)
    terms = lax.all_gather(mul(lower, later_low), "row")[1] * first
    value = value - sum_scatter(mul_t(inverse, terms, precision=fine), "col", COLS)
    return value[None], root_part


def solution(mesh):
    return jax.shard_map(
        shards,
        mesh=mesh,
        in_specs=(
            P("sub", None, "col", "row"),
            P("sub", None, None),
            P("sub", ("row", "col"), None),
            P("sub", "row", "col", None),
            P("sub", None),
            P("col", None),
            P("sub", "row", None),
            P("col", None),
        ),
        out_specs=(P("sub", ("row", "col"), None), P("col", None)),
        check_vma=False,
    )
```

```python
import jax
import jax.numpy as jnp
from jax import lax
from jax.sharding import PartitionSpec as P

BLOCK = 256
PANEL = 2048
SEPARATOR = 1536
COLS = 16
SUBS = 8

f32 = jnp.float32
bf16 = jnp.bfloat16
fine = lax.Precision.HIGH
first_axes = (((0,), (0,)), ((), ()))


def mul(left, right, **kw):
    return jnp.dot(left, right, preferred_element_type=f32, **kw)


def mul_t(left, right, **kw):
    return lax.dot_general(left, right, first_axes, preferred_element_type=f32, **kw)


def after(value, other):
    return lax.optimization_barrier((value, other))[0]


def collect(blocks, step, sub_id):
    other = lax.ppermute(blocks, "sub", [(i, i ^ step) for i in range(SUBS)])
    return jnp.where(
        sub_id & step == 0,
        jnp.concatenate([blocks, other], 0),
        jnp.concatenate([other, blocks], 0),
    )


def sum_scatter(partial, axes, count):
    parts = partial.reshape(count, -1, partial.shape[-1])
    here = lax.axis_index(axes)
    own = lax.dynamic_index_in_dim(parts, here, 0)
    low, own = lax.optimization_barrier((parts.astype(bf16), own))
    others = lax.all_to_all(low, axes, 0, 0).astype(f32)
    index = lax.broadcasted_iota(jnp.int32, (count, 1, 1), 0)
    return jnp.where(index == here, own, others).sum(0)


def gather(chunk, axes, count):
    spread = jnp.broadcast_to(chunk[None], (count,) + chunk.shape)
    return lax.all_to_all(spread, axes, 0, 0)


def shards(
    factor_cols,
    block_pattern,
    diag_inverse,
    coupling_cols,
    separator_rows,
    root_inverse,
    right_side,
    root_right,
):
    table = block_pattern[0]
    inverse = diag_inverse[0]
    couple = coupling_cols[0, 0]
    rows_sep = separator_rows[0]
    row_id = lax.axis_index("row")
    col_id = lax.axis_index("col")
    sources = right_side.shape[-1]
    sub_id = lax.axis_index("sub")
    band_id = row_id * SUBS + sub_id % 2 * 4 + sub_id // 2 % 2 * 2 + sub_id // 4

    blocks = lax.dynamic_slice(table, (PANEL // BLOCK, col_id // 2), (PANEL // BLOCK, 1))
    lower = factor_cols[0, 0] * jnp.repeat(blocks[:, 0], BLOCK)[None, :].astype(bf16)
    width = lower.shape[0]

    own = mul(inverse, right_side[0], precision=fine)
    first_low = lax.ppermute(own.astype(bf16), "row", [(0, 1)])
    partial = mul_t(lower, first_low).astype(bf16)

    share = root_inverse.shape[0]
    band = SEPARATOR // (2 * SUBS)
    gram = mul_t(
        root_inverse,
        lax.dynamic_slice_in_dim(root_inverse, band_id * band, band, 1),
        precision=fine,
    ).reshape(COLS, share, band)
    own_gram = lax.dynamic_index_in_dim(gram, col_id, 0)
    gram = jnp.pad(gram.astype(bf16), ((0, 0), (0, 0), (0, sources - band)))

    chunk = share // 2
    pairs = [
        (core * COLS + chip, (chip // 8) * COLS + 2 * (chip % 8) + core)
        for core in range(2)
        for chip in range(COLS)
    ]
    root_rows = lax.dynamic_slice_in_dim(after(root_right, partial), row_id * chunk, chunk, 0)
    root_rows = lax.ppermute(root_rows, ("row", "col"), pairs)

    onehot = (jnp.arange(SEPARATOR)[:, None] == after(rows_sep, partial)[None, :]).astype(bf16)
    couple_sep = lax.dot_general(
        onehot, couple, (((1,), (1,)), ((), ())), preferred_element_type=f32
    ).astype(bf16)

    both = jnp.concatenate([partial.reshape(COLS, width, sources), gram], 1)
    both = after(lax.all_to_all(both, "col", 0, 0), (root_rows, couple_sep))
    total = both[:, :width].astype(f32).sum(0).astype(bf16)
    chips = lax.broadcasted_iota(jnp.int32, (COLS, 1, 1), 0)
    gram = jnp.where(chips == col_id, own_gram, both[:, width:, :band].astype(f32)).sum(0)
    gram = collect(gram.T, 4, sub_id)

    total = after(gather(total, "col", COLS), gram).reshape(PANEL, sources)
    solved = own - mul(inverse, total.astype(f32), precision=fine)

    gram = collect(gram, 2, sub_id)
    updates = mul(couple_sep, solved.astype(bf16)).astype(bf16).reshape(2 * COLS, chunk, sources)
    updates = after(lax.all_to_all(updates, ("row", "col"), 0, 0), gram)
    updates = updates.astype(f32).sum(0)
    updates = gather(updates, "sub", SUBS).sum(0)
    gram = collect(after(gram, updates), 1, sub_id)
    gram, first = lax.optimization_barrier((gram, (row_id == 0).astype(f32)))
    rhs = gather(root_rows - updates, "col", COLS).reshape(SEPARATOR // 2, sources)
    root_part = lax.all_gather(mul_t(gram, rhs, precision=fine), "row").sum(0)
    root_full = gather(root_part.astype(bf16), "col", COLS).reshape(SEPARATOR, sources)
    value = solved - mul_t(couple_sep, root_full)

    value = sum_scatter(mul_t(inverse, value, precision=fine), "col", COLS)
    later_low = gather(value.astype(bf16), "col", COLS).reshape(PANEL, sources)
    terms = lax.all_gather(mul(lower, later_low), "row")[1] * first
    value = value - sum_scatter(mul_t(inverse, terms, precision=fine), "col", COLS)
    return value[None], root_part


def solution(mesh):
    return jax.shard_map(
        shards,
        mesh=mesh,
        in_specs=(
            P("sub", None, "col", "row"),
            P("sub", None, None),
            P("sub", ("row", "col"), None),
            P("sub", "row", "col", None),
            P("sub", None),
            P("col", None),
            P("sub", "row", None),
            P("col", None),
        ),
        out_specs=(P("sub", ("row", "col"), None), P("col", None)),
        check_vma=False,
    )
```
